256 devices in a mesh: dp: 16 (over y, z_hi), tensor: 16 (over z_lo, x, core).
Axes of the slice: x: 4, y: 4, z: 8 (z_hi: 4, z_lo: 2; z = z_hi * 2 + z_lo), core: 2. Of those that a mesh axis runs over, the one named last changes fastest.
Arguments:
- tokens: bfloat16 [768, 8192], P('tensor', 'dp'), may hold values from -6 to 6
- w_gate: bfloat16 [8192, 28672], P('dp', 'tensor'), may hold values from -0.0625 to 0.0625
- w_up: bfloat16 [8192, 28672], P('dp', 'tensor'), may hold values from -0.0625 to 0.0625
- w_down: bfloat16 [28672, 8192], P('tensor', 'dp'), may hold values from -0.03125 to 0.03125
- cotangent: bfloat16 [768, 8192], P('tensor', 'dp'), may hold values from -6 to 6
Outputs:
- d_tokens: bfloat16 [768, 8192], P('tensor', 'dp')
- d_gate: bfloat16 [8192, 28672], P('dp', 'tensor')
- d_up: bfloat16 [8192, 28672], P('dp', 'tensor')
- d_down: bfloat16 [28672, 8192], P('tensor', 'dp')
The draws below stay inside these ranges and needn't reach their ends.
All inputs are finite; a program needn't handle non-finite values.
Results may differ from the reference program's by a relative error of at most 0.0057.
Values may be sent and summed in bfloat16 or wider, within the bound.
A program may use at most 128 MiB of HBM per device.

```python
import math
import jax
import jax.numpy as jnp
from jax import lax

D = 8192
F = 28672
BLK = 128
TOKENS = 768
N_TENSOR = 16


def level_of(key, dims, cuts, low, high):
    level = 1.0
    for dim, blocks in cuts:
        heights = jax.random.uniform(jax.random.fold_in(jax.random.fold_in(key, 6), dim), (blocks,), jnp.float32, low / len(cuts), high / len(cuts))
        level = level * jnp.repeat(jnp.exp(heights), dims[dim] // blocks).reshape((-1,) + (1,) * (len(dims) - 1 - dim))
    return level


def gaussian(key, dims, width, limit, shards=(), kind=jnp.bfloat16):
    level = level_of(key, dims, shards, -0.22, 0.18) if shards else 1.0
    values = jax.random.normal(key, dims, jnp.float32) * width * level
    return jnp.minimum(jnp.maximum(values, -limit), limit).astype(kind)


def setup_inputs(seed: int = 0) -> dict:
    streams_of = jax.random.split(jax.random.key(seed), 6)
    tokens = gaussian(streams_of[0], (TOKENS, D), 1.0, 6.0, ((0, 16), (1, 16)))
    w_gate = gaussian(streams_of[1], (D, F), D ** -0.5, 0.0625, ((0, 16), (1, 16)))
    w_up = gaussian(streams_of[2], (D, F), D ** -0.5, 0.0625, ((0, 16), (1, 16)))
    w_down = gaussian(streams_of[3], (F, D), F ** -0.5, 0.03125, ((0, 16), (1, 16)))
    cotangent = gaussian(streams_of[4], (TOKENS, D), 1.0, 6.0, ((0, 16), (1, 16)))
    return {"tokens": tokens, "w_gate": w_gate, "w_up": w_up, "w_down": w_down, "cotangent": cotangent}


def sylvester(order):
    positions = jnp.arange(order, dtype=jnp.int32)
    row_ids = positions[:, None]
    col_ids = positions[None, :]
    signs = jnp.ones((order, order), jnp.float32)
    for power in range(order.bit_length() - 1):
        both = (row_ids >> power & 1) * (col_ids >> power & 1)
        signs = signs * (1 - 2 * both).astype(jnp.float32)
    return signs

def rotate(values):
    row_count = values.shape[0]
    shaped = values.reshape(row_count, N_TENSOR, F // N_TENSOR // BLK, BLK)
    inner = jnp.einsum('mtbj,jk->mtbk', shaped, sylvester(BLK), precision=lax.Precision.HIGHEST)
    outer = jnp.einsum('st,mtbk->msbk', sylvester(N_TENSOR), inner, precision=lax.Precision.HIGHEST)
    return outer.reshape(row_count, F) * (1.0 / math.sqrt(BLK * N_TENSOR))

def reference(tokens, w_gate, w_up, w_down, cotangent):
    gate = jnp.dot(tokens, w_gate, preferred_element_type=jnp.float32)
    up = jnp.dot(tokens, w_up, preferred_element_type=jnp.float32)
    sigma = jax.nn.sigmoid(gate)
    silu_gate = gate * sigma
    hidden = (silu_gate * up).astype(jnp.bfloat16)
    rotated = rotate(hidden.astype(jnp.float32)).astype(jnp.bfloat16)
    d_down = jnp.dot(rotated.T, cotangent, preferred_element_type=jnp.float32).astype(jnp.bfloat16)
    d_rotated = jnp.dot(cotangent, w_down.T, preferred_element_type=jnp.float32)
    d_hidden = rotate(d_rotated)
    d_gate_pre = (d_hidden * up * sigma * (1.0 + gate * (1.0 - sigma))).astype(jnp.bfloat16)
    d_up_pre = (d_hidden * silu_gate).astype(jnp.bfloat16)
    d_gate = jnp.dot(tokens.T, d_gate_pre, preferred_element_type=jnp.float32).astype(jnp.bfloat16)
    d_up = jnp.dot(tokens.T, d_up_pre, preferred_element_type=jnp.float32).astype(jnp.bfloat16)
    d_tokens = (jnp.dot(d_gate_pre, w_gate.T, preferred_element_type=jnp.float32) + jnp.dot(d_up_pre, w_up.T, preferred_element_type=jnp.float32)).astype(jnp.bfloat16)
    return (d_tokens, d_gate, d_up, d_down)
```

```python
import functools
import math

import jax
import jax.numpy as jnp
from jax import lax
from jax.experimental import pallas as pl
from jax.experimental.pallas import tpu as pltpu
from jax.sharding import PartitionSpec as P

BLK = 128
BF = jnp.bfloat16
F32 = jnp.float32
MESH = pl.DeviceIdType.MESH
NQ = 7
NP = 3 * NQ
LAG_B, LAG_C, LAG_D, LAG_E = 1, 3, 4, 5
ROT_0 = NQ + LAG_E


def swapped(value, axis, distance):
    mask = 2**distance
    pairs = [(source, source ^ mask) for source in range(lax.axis_size(axis))]
    return lax.ppermute(value, axis, pairs)


def sylvester(order, dtype=jnp.float32):
    positions = jnp.arange(order, dtype=jnp.int32)
    row_ids = positions[:, None]
    col_ids = positions[None, :]
    signs = jnp.ones((order, order), jnp.float32)
    for power in range(order.bit_length() - 1):
        both = (row_ids >> power & 1) * (col_ids >> power & 1)
        signs = signs * (1 - 2 * both).astype(jnp.float32)
    return signs.astype(dtype)


def rotate(values):
    row_count, width = values.shape
    shaped = values.reshape(row_count, width // BLK, BLK)
    inner = jnp.einsum("mbj,jk->mbk", shaped, sylvester(BLK), precision=lax.Precision.HIGHEST)
    inner = inner.reshape(row_count, width)
    members = lax.axis_size("tensor")
    position = lax.axis_index("tensor")
    mixed = inner
    for power in range(members.bit_length() - 1):
        partner = swapped(mixed, "tensor", power)
        upper = position >> power & 1 == 1
        mixed = jnp.where(upper, partner - mixed, mixed + partner)
    return mixed * (1.0 / math.sqrt(BLK * members))


class Place:
    def __init__(self):
        self.dp = lax.axis_index("dp")
        self.t = lax.axis_index("tensor")
        self.y, self.zh = lax.div(self.dp, 4), lax.rem(self.dp, 4)
        self.zl = lax.div(self.t, 8)
        self.x = lax.rem(lax.div(self.t, 2), 4)
        self.core = lax.rem(self.t, 2)

    def at_y(self, step):
        return lax.rem(self.y + step + 4, 4)

    def at_z(self, step):
        return lax.rem(self.zh + step + 4, 4)

    def at_x(self, step):
        return lax.rem(self.x + step + 4, 4)

    def dp_y(self, step):
        return {"dp": self.at_y(step) * 4 + self.zh, "tensor": self.t}

    def dp_z(self, step):
        return {"dp": self.y * 4 + self.at_z(step), "tensor": self.t}

    def slot(self, zl, x, core):
        return zl * 8 + x * 2 + core

    def to_x(self, step):
        return {"dp": self.dp, "tensor": self.slot(self.zl, self.at_x(step), self.core)}

    def to_core(self):
        return {"dp": self.dp, "tensor": self.slot(self.zl, self.x, 1 - self.core)}

    def to_zl(self):
        return {"dp": self.dp, "tensor": self.slot(1 - self.zl, self.x, self.core)}

    def meet(self):
        peers = [self.dp_y(1), self.dp_y(-1), self.dp_z(1), self.dp_z(-1)]
        peers += [self.to_x(k) for k in (1, 2, 3)] + [self.to_core(), self.to_zl()]
        barrier = pltpu.get_barrier_semaphore()
        for peer in peers:
            pl.semaphore_signal(barrier, inc=1, device_id=peer, device_id_type=MESH)
        pl.semaphore_wait(barrier, len(peers))


def send(src, dst, send_sem, recv_sem, to):
    return pltpu.make_async_remote_copy(
        src_ref=src, dst_ref=dst, send_sem=send_sem, recv_sem=recv_sem, device_id=to, device_id_type=MESH
    )


def sign_of(bit):
    return (1 - 2 * bit).astype(F32)


def x_sign(place, other):
    both = lax.rem(place.x, 2) * lax.rem(other, 2) + lax.div(place.x, 2) * lax.div(other, 2)
    return sign_of(lax.rem(both, 2))


def inner_hadamard(value, had):
    parts = []
    for start in range(0, value.shape[1], BLK):
        block = value[:, start : start + BLK]
        high = block.astype(BF)
        low = (block - high.astype(F32)).astype(BF)
        parts.append(
            jnp.dot(high, had, preferred_element_type=F32) + jnp.dot(low, had, preferred_element_type=F32)
        )
    return jnp.concatenate(parts, axis=1)


def reduce_kernel(
    tok, cot, wg, wu, wd, had,
    X, GU, DH,
    W, WD, s1s, s1r, s2s, s2r, T, z1s, z1r, z2s, z2r, RA, RX, RB, RC, RD, RE,
    load_sem, gz, gx, gc, gs, s1_out, s1_in, s2_out, s2_in, z1_out, z1_in, z2_out, z2_in, rx_in, r_in, r_out,
):
    me = Place()
    loads = [pltpu.make_async_copy(wd, WD, load_sem.at[0])]
    for q in range(NQ):
        loads.append(pltpu.make_async_copy(wg.at[:, pl.ds(256 * q, 256)], W.at[NQ + q], load_sem.at[1 + q]))
        loads.append(pltpu.make_async_copy(wu.at[:, pl.ds(256 * q, 256)], W.at[2 * NQ + q], load_sem.at[1 + NQ + q]))
    for load in loads:
        load.start()
    me.meet()

    other = me.slot(1 - me.zl, me.x, me.core)

    def gather_own(s, own):
        X[s, me.t] = own[...]
        send(X.at[s, me.t], X.at[s, me.t], gs.at[s], gz.at[s], me.to_zl()).start()
        for k in (1, 2, 3):
            send(X.at[s, me.t], X.at[s, me.t], gs.at[s], gx.at[s, 0, k - 1], me.to_x(k)).start()

    def gather_zl(s):
        send(X.at[s, other], X.at[s, other], gs.at[s], gz.at[s], me.to_zl()).wait_recv()
        for k in (1, 2, 3):
            send(X.at[s, other], X.at[s, other], gs.at[s], gx.at[s, 1, k - 1], me.to_x(k)).start()

    def to_core(s, zl, x, n):
        block = X.at[s, me.slot(zl, x, me.core)]
        send(block, block, gs.at[s], gc.at[s, n], me.to_core()).start()

    def gather_x(s):
        to_core(s, me.zl, me.x, 0)
        to_core(s, 1 - me.zl, me.x, 4)
        for j, zl in ((0, me.zl), (1, 1 - me.zl)):
            for k in (1, 2, 3):
                came = me.at_x(-k)
                block = X.at[s, me.slot(zl, came, me.core)]
                send(block, block, gs.at[s], gx.at[s, j, k - 1], me.to_x(k)).wait_recv()
                to_core(s, zl, came, 4 * j + k)

    def gather_core(s):
        for j, zl in ((0, me.zl), (1, 1 - me.zl)):
            for k in range(4):
                block = X.at[s, me.slot(zl, me.at_x(-k), 1 - me.core)]
                send(block, block, gs.at[s], gc.at[s, 4 * j + k], me.to_core()).wait_recv()

    gather_own(0, cot)
    gather_own(1, tok)
    loads[0].wait()
    for q in range(NQ):
        W[q] = WD[pl.ds(256 * q, 256), :].T
    gather_zl(0)
    gather_zl(1)
    gather_x(0)
    gather_core(0)
    for load in loads[1:]:
        load.wait()

    def partial(p, chunk):
        s = jnp.where(p < NQ, 0, 1)
        rows = X[s, pl.ds(4 * chunk, 4)].reshape(192, 512)
        return jnp.dot(rows, W[p], preferred_element_type=F32)

    def s1(p, way):
        return send(s1s.at[p, way], s1r.at[p, way], s1_out, s1_in.at[p, way], me.dp_y(1 - 2 * way))

    def s2(p, way):
        return send(s2s.at[p, way], s2r.at[p, way], s2_out, s2_in.at[p, way], me.dp_y(1 - 2 * way))

    def z1(p, way):
        return send(z1s.at[p, way], z1r.at[p, way], z1_out, z1_in.at[p, way], me.dp_z(1 - 2 * way))

    def z2(p, way):
        return send(z2s.at[p, way], z2r.at[p, way], z2_out, z2_in.at[p, way], me.dp_z(1 - 2 * way))

    def stage_a(p):
        far = partial(p, me.at_y(2)).astype(BF)
        for way in (0, 1):
            s1s[p, way] = far[:, 128 * way : 128 * way + 128]
            s1(p, way).start()

    def stage_b(p):
        for way in (0, 1):
            near = partial(p, me.at_y(1 - 2 * way))
            s1(p, way).wait_recv()
            for half in (0, 1):
                value = near[:, 128 * half : 128 * half + 128]
                if half == way:
                    value = value + s1r[p, way].astype(F32)
                s2s[p, way, half] = value.astype(BF)
            s2(p, way).start()

    def stage_c(p):
        own = partial(p, me.y)
        s2(p, 0).wait_recv()
        s2(p, 1).wait_recv()
        for half in (0, 1):
            value = own[:, 128 * half : 128 * half + 128]
            value = value + s2r[p, 0, half].astype(F32) + s2r[p, 1, half].astype(F32)
            T[p, half] = value.reshape(4, 48, 128)
        for way in (0, 1):
            z1s[p, way] = T[p, way, me.at_z(2)].astype(BF)
            z1(p, way).start()

    def stage_d(p):
        for way in (0, 1):
            z1(p, way).wait_recv()
            for half in (0, 1):
                value = T[p, half, me.at_z(1 - 2 * way)]
                if half == way:
                    value = value + z1r[p, way].astype(F32)
                z2s[p, way, half] = value.astype(BF)
            z2(p, way).start()

    def stage_e(p):
        z2(p, 0).wait_recv()
        z2(p, 1).wait_recv()
        halves = [
            T[p, half, me.zh] + z2r[p, 0, half].astype(F32) + z2r[p, 1, half].astype(F32) for half in (0, 1)
        ]
        total = jnp.concatenate(halves, axis=1)

        @pl.when(p < NQ)
        def _():
            RA[p] = inner_hadamard(total, had[...])

        @pl.when(p >= NQ)
        def _():
            GU[p - NQ] = total

    def rx(k):
        return send(RA, RX.at[k - 1], r_out.at[k - 1], rx_in.at[k - 1], me.to_x(k))

    rc = send(RB, RC, r_out.at[3], r_in.at[0], me.to_core())
    rz = send(RD, RE, r_out.at[4], r_in.at[1], me.to_zl())

    def rotate_0():
        for k in (1, 2, 3):
            rx(k).start()

    def rotate_1():
        for k in (1, 2, 3):
            rx(k).wait_recv()

        @pl.loop(0, NQ)
        def _(q):
            total = x_sign(me, me.x) * RA[q]
            for k in (1, 2, 3):
                total = total + x_sign(me, me.at_x(-k)) * RX[k - 1, q]
            RB[q] = total

        rc.start()

    def rotate_2():
        rc.wait_recv()

        @pl.loop(0, NQ)
        def _(q):
            RD[q] = RC[q] + sign_of(me.core) * RB[q]

        rz.start()

    def rotate_3():
        rz.wait_recv()

        @pl.loop(0, NQ)
        def _(q):
            DH[q] = (RE[q] + sign_of(me.zl) * RD[q]) * (1.0 / math.sqrt(BLK * 16))

    @pl.loop(0, NP + LAG_E)
    def _(i):
        @pl.when(i == 1)
        def _():
            gather_x(1)

        @pl.when(i == 3)
        def _():
            gather_core(1)

        @pl.when(i == ROT_0)
        def _():
            rotate_0()

        @pl.when(i == ROT_0 + 6)
        def _():
            rotate_1()

        @pl.when(i == ROT_0 + 8)
        def _():
            rotate_2()

        for stage, lag in ((stage_a, 0), (stage_b, LAG_B), (stage_c, LAG_C), (stage_d, LAG_D), (stage_e, LAG_E)):

            @pl.when((i >= lag) & (i < NP + lag))
            def _(stage=stage, lag=lag):
                stage(i - lag)

    rotate_3()
    for s in (0, 1):
        sent = X.at[s, pl.ds(0, 15)]
        send(sent, sent, gs.at[s], gz.at[s], me.to_zl()).wait_send()
    send(s1s, s1r, s1_out, s1_in.at[0, 0], me.dp_y(1)).wait_send()
    send(s2s, s2r, s2_out, s2_in.at[0, 0], me.dp_y(1)).wait_send()
    send(z1s, z1r, z1_out, z1_in.at[0, 0], me.dp_z(1)).wait_send()
    send(z2s, z2r, z2_out, z2_in.at[0, 0], me.dp_z(1)).wait_send()
    for k in (1, 2, 3):
        rx(k).wait_send()
    rc.wait_send()
    rz.wait_send()


def reduce_phase(tokens, cotangent, w_gate, w_up, w_down):
    whole = pl.BlockSpec(memory_space=pltpu.VMEM)
    any_space = pl.BlockSpec(memory_space=pl.ANY)
    dma = pltpu.SemaphoreType.DMA
    rot = pltpu.VMEM((NQ, 48, 256), F32)
    return pl.pallas_call(
        reduce_kernel,
        out_shape=(
            jax.ShapeDtypeStruct((2, 16, 48, 512), BF),
            jax.ShapeDtypeStruct((2 * NQ, 48, 256), F32),
            jax.ShapeDtypeStruct((NQ, 48, 256), F32),
        ),
        in_specs=[whole, whole, any_space, any_space, any_space, whole],
        out_specs=(whole, whole, whole),
        scratch_shapes=[
            pltpu.VMEM((NP, 512, 256), BF),
            pltpu.VMEM((1792, 512), BF),
            pltpu.VMEM((NP, 2, 192, 128), BF),
            pltpu.VMEM((NP, 2, 192, 128), BF),
            pltpu.VMEM((NP, 2, 2, 192, 128), BF),
            pltpu.VMEM((NP, 2, 2, 192, 128), BF),
            pltpu.VMEM((NP, 2, 4, 48, 128), F32),
            pltpu.VMEM((NP, 2, 48, 128), BF),
            pltpu.VMEM((NP, 2, 48, 128), BF),
            pltpu.VMEM((NP, 2, 2, 48, 128), BF),
            pltpu.VMEM((NP, 2, 2, 48, 128), BF),
            rot, pltpu.VMEM((3, NQ, 48, 256), F32), rot, rot, rot, rot,
            dma((15,)), dma((2,)), dma((2, 2, 3)), dma((2, 8)), dma((2,)),
            dma, dma((NP, 2)), dma, dma((NP, 2)), dma, dma((NP, 2)), dma, dma((NP, 2)),
            dma((3,)), dma((2,)), dma((5,)),
        ],
        compiler_params=pltpu.CompilerParams(
            collective_id=0, has_side_effects=True, vmem_limit_bytes=56 * 1024 * 1024
        ),
        name="reduce_phase",
    )(tokens, cotangent, w_gate, w_up, w_down, sylvester(BLK, BF))


def per_device(tokens, w_gate, w_up, w_down, cotangent):
    X, GU, DH = reduce_phase(tokens, cotangent, w_gate, w_up, w_down)
    all_cotangent, all_tokens = X[0].reshape(768, 512), X[1].reshape(768, 512)
    gate = GU[:NQ].transpose(1, 0, 2).reshape(48, 1792)
    up = GU[NQ:].transpose(1, 0, 2).reshape(48, 1792)
    d_hidden = DH.transpose(1, 0, 2).reshape(48, 1792)
    sigma = jax.nn.sigmoid(gate)
    silu_gate = gate * sigma
    hidden = (silu_gate * up).astype(jnp.bfloat16)
    rotated = rotate(hidden.astype(jnp.float32)).astype(jnp.bfloat16)
    block_rows = all_cotangent
    d_down = lax.dot_general(
        lax.all_gather(rotated, "dp", axis=0, tiled=True),
        block_rows,
        (((0,), (0,)), ((), ())),
        preferred_element_type=jnp.float32,
    ).astype(jnp.bfloat16)
    d_gate_pre = (d_hidden * up * sigma * (1.0 + gate * (1.0 - sigma))).astype(jnp.bfloat16)
    d_up_pre = (d_hidden * silu_gate).astype(jnp.bfloat16)
    grads_gate, grads_up = (
        lax.all_gather(d_gate_pre, "dp", axis=0, tiled=True),
        lax.all_gather(d_up_pre, "dp", axis=0, tiled=True),
    )
    contract_rows = (((0,), (0,)), ((), ()))
    d_gate = lax.dot_general(
        all_tokens, grads_gate, contract_rows, preferred_element_type=jnp.float32
    ).astype(jnp.bfloat16)
    d_up = lax.dot_general(
        all_tokens, grads_up, contract_rows, preferred_element_type=jnp.float32
    ).astype(jnp.bfloat16)
    contract_cols = (((1,), (1,)), ((), ()))
    first = lax.dot_general(grads_gate, w_gate, contract_cols, preferred_element_type=jnp.float32)
    second = lax.dot_general(grads_up, w_up, contract_cols, preferred_element_type=jnp.float32)
    d_tokens = lax.psum_scatter(first + second, "tensor", scatter_dimension=0, tiled=True).astype(
        jnp.bfloat16
    )
    return (d_tokens, d_gate, d_up, d_down)


def solution(mesh):
    return jax.shard_map(
        per_device,
        mesh=mesh,
        in_specs=(
            P("tensor", "dp"),
            P("dp", "tensor"),
            P("dp", "tensor"),
            P("tensor", "dp"),
            P("tensor", "dp"),
        ),
        out_specs=(P("tensor", "dp"), P("dp", "tensor"), P("dp", "tensor"), P("tensor", "dp")),
        check_vma=False,
    )
```

```python
import functools
import math

import jax
import jax.numpy as jnp
from jax import lax
from jax.experimental import pallas as pl
from jax.experimental.pallas import tpu as pltpu
from jax.sharding import PartitionSpec as P

BLK = 128
BF = jnp.bfloat16
F32 = jnp.float32
MESH = pl.DeviceIdType.MESH
NQ = 7
NP = 3 * NQ
LAG_B, LAG_C, LAG_D, LAG_E = 1, 3, 4, 5
ROT_0 = NQ + LAG_E


def sylvester(order, dtype=jnp.float32):
    positions = jnp.arange(order, dtype=jnp.int32)
    row_ids = positions[:, None]
    col_ids = positions[None, :]
    signs = jnp.ones((order, order), jnp.float32)
    for power in range(order.bit_length() - 1):
        both = (row_ids >> power & 1) * (col_ids >> power & 1)
        signs = signs * (1 - 2 * both).astype(jnp.float32)
    return signs.astype(dtype)


class Place:
    def __init__(self):
        self.dp = lax.axis_index("dp")
        self.t = lax.axis_index("tensor")
        self.y, self.zh = lax.div(self.dp, 4), lax.rem(self.dp, 4)
        self.zl = lax.div(self.t, 8)
        self.x = lax.rem(lax.div(self.t, 2), 4)
        self.core = lax.rem(self.t, 2)

    def at_y(self, step):
        return lax.rem(self.y + step + 4, 4)

    def at_z(self, step):
        return lax.rem(self.zh + step + 4, 4)

    def at_x(self, step):
        return lax.rem(self.x + step + 4, 4)

    def dp_y(self, step):
        return {"dp": self.at_y(step) * 4 + self.zh, "tensor": self.t}

    def dp_z(self, step):
        return {"dp": self.y * 4 + self.at_z(step), "tensor": self.t}

    def slot(self, zl, x, core):
        return zl * 8 + x * 2 + core

    def to_x(self, step):
        return {"dp": self.dp, "tensor": self.slot(self.zl, self.at_x(step), self.core)}

    def to_core(self):
        return {"dp": self.dp, "tensor": self.slot(self.zl, self.x, 1 - self.core)}

    def to_zl(self):
        return {"dp": self.dp, "tensor": self.slot(1 - self.zl, self.x, self.core)}

    def meet(self):
        peers = [self.dp_y(1), self.dp_y(-1), self.dp_z(1), self.dp_z(-1)]
        peers += [self.to_x(k) for k in (1, 2, 3)] + [self.to_core(), self.to_zl()]
        barrier = pltpu.get_barrier_semaphore()
        for peer in peers:
            pl.semaphore_signal(barrier, inc=1, device_id=peer, device_id_type=MESH)
        pl.semaphore_wait(barrier, len(peers))


def send(src, dst, send_sem, recv_sem, to):
    return pltpu.make_async_remote_copy(
        src_ref=src, dst_ref=dst, send_sem=send_sem, recv_sem=recv_sem, device_id=to, device_id_type=MESH
    )


def sign_of(bit):
    return (1 - 2 * bit).astype(F32)


def x_sign(place, other):
    both = lax.rem(place.x, 2) * lax.rem(other, 2) + lax.div(place.x, 2) * lax.div(other, 2)
    return sign_of(lax.rem(both, 2))


def inner_hadamard(value, had):
    parts = []
    for start in range(0, value.shape[1], BLK):
        block = value[:, start : start + BLK]
        high = block.astype(BF)
        low = (block - high.astype(F32)).astype(BF)
        parts.append(
            jnp.dot(high, had, preferred_element_type=F32) + jnp.dot(low, had, preferred_element_type=F32)
        )
    return jnp.concatenate(parts, axis=1)


def reduce_kernel(
    tok, cot, wg, wu, wd, had,
    X, GU, DH,
    W, WD, s1s, s1r, s2s, s2r, T, z1s, z1r, z2s, z2r, RA, RX, RB, RC, RD, RE,
    load_sem, gz, gx, gc, gs, s1_out, s1_in, s2_out, s2_in, z1_out, z1_in, z2_out, z2_in, rx_in, r_in, r_out,
):
    me = Place()
    loads = [pltpu.make_async_copy(wd, WD, load_sem.at[0])]
    for q in range(NQ):
        loads.append(pltpu.make_async_copy(wg.at[:, pl.ds(256 * q, 256)], W.at[NQ + q], load_sem.at[1 + q]))
        loads.append(pltpu.make_async_copy(wu.at[:, pl.ds(256 * q, 256)], W.at[2 * NQ + q], load_sem.at[1 + NQ + q]))
    for load in loads:
        load.start()
    me.meet()

    other = me.slot(1 - me.zl, me.x, me.core)

    def gather_own(s, own):
        X[s, me.t] = own[...]
        send(X.at[s, me.t], X.at[s, me.t], gs.at[s], gz.at[s], me.to_zl()).start()
        for k in (1, 2, 3):
            send(X.at[s, me.t], X.at[s, me.t], gs.at[s], gx.at[s, 0, k - 1], me.to_x(k)).start()

    def gather_zl(s):
        send(X.at[s, other], X.at[s, other], gs.at[s], gz.at[s], me.to_zl()).wait_recv()
        for k in (1, 2, 3):
            send(X.at[s, other], X.at[s, other], gs.at[s], gx.at[s, 1, k - 1], me.to_x(k)).start()

    def to_core(s, zl, x, n):
        block = X.at[s, me.slot(zl, x, me.core)]
        send(block, block, gs.at[s], gc.at[s, n], me.to_core()).start()

    def gather_x(s):
        to_core(s, me.zl, me.x, 0)
        to_core(s, 1 - me.zl, me.x, 4)
        for j, zl in ((0, me.zl), (1, 1 - me.zl)):
            for k in (1, 2, 3):
                came = me.at_x(-k)
                block = X.at[s, me.slot(zl, came, me.core)]
                send(block, block, gs.at[s], gx.at[s, j, k - 1], me.to_x(k)).wait_recv()
                to_core(s, zl, came, 4 * j + k)

    def gather_core(s):
        for j, zl in ((0, me.zl), (1, 1 - me.zl)):
            for k in range(4):
                block = X.at[s, me.slot(zl, me.at_x(-k), 1 - me.core)]
                send(block, block, gs.at[s], gc.at[s, 4 * j + k], me.to_core()).wait_recv()

    gather_own(0, cot)
    gather_own(1, tok)
    loads[0].wait()
    for q in range(NQ):
        W[q] = WD[pl.ds(256 * q, 256), :].T
    gather_zl(0)
    gather_zl(1)
    gather_x(0)
    gather_core(0)
    for load in loads[1:]:
        load.wait()

    def partial(p, chunk):
        s = jnp.where(p < NQ, 0, 1)
        rows = X[s, pl.ds(4 * chunk, 4)].reshape(192, 512)
        return jnp.dot(rows, W[p], preferred_element_type=F32)

    def s1(p, way):
        return send(s1s.at[p, way], s1r.at[p, way], s1_out, s1_in.at[p, way], me.dp_y(1 - 2 * way))

    def s2(p, way):
        return send(s2s.at[p, way], s2r.at[p, way], s2_out, s2_in.at[p, way], me.dp_y(1 - 2 * way))

    def z1(p, way):
        return send(z1s.at[p, way], z1r.at[p, way], z1_out, z1_in.at[p, way], me.dp_z(1 - 2 * way))

    def z2(p, way):
        return send(z2s.at[p, way], z2r.at[p, way], z2_out, z2_in.at[p, way], me.dp_z(1 - 2 * way))

    def stage_a(p):
        far = partial(p, me.at_y(2)).astype(BF)
        for way in (0, 1):
            s1s[p, way] = far[:, 128 * way : 128 * way + 128]
            s1(p, way).start()

    def stage_b(p):
        for way in (0, 1):
            near = partial(p, me.at_y(1 - 2 * way))
            s1(p, way).wait_recv()
            for half in (0, 1):
                value = near[:, 128 * half : 128 * half + 128]
                if half == way:
                    value = value + s1r[p, way].astype(F32)
                s2s[p, way, half] = value.astype(BF)
            s2(p, way).start()

    def stage_c(p):
        own = partial(p, me.y)
        s2(p, 0).wait_recv()
        s2(p, 1).wait_recv()
        for half in (0, 1):
            value = own[:, 128 * half : 128 * half + 128]
            value = value + s2r[p, 0, half].astype(F32) + s2r[p, 1, half].astype(F32)
            T[p, half] = value.reshape(4, 48, 128)
        for way in (0, 1):
            z1s[p, way] = T[p, way, me.at_z(2)].astype(BF)
            z1(p, way).start()

    def stage_d(p):
        for way in (0, 1):
            z1(p, way).wait_recv()
            for half in (0, 1):
                value = T[p, half, me.at_z(1 - 2 * way)]
                if half == way:
                    value = value + z1r[p, way].astype(F32)
                z2s[p, way, half] = value.astype(BF)
            z2(p, way).start()

    def stage_e(p):
        z2(p, 0).wait_recv()
        z2(p, 1).wait_recv()
        halves = [
            T[p, half, me.zh] + z2r[p, 0, half].astype(F32) + z2r[p, 1, half].astype(F32) for half in (0, 1)
        ]
        total = jnp.concatenate(halves, axis=1)

        @pl.when(p < NQ)
        def _():
            RA[p] = inner_hadamard(total, had[...])

        @pl.when(p >= NQ)
        def _():
            GU[p - NQ] = total

    def rx(k):
        return send(RA, RX.at[k - 1], r_out.at[k - 1], rx_in.at[k - 1], me.to_x(k))

    rc = send(RB, RC, r_out.at[3], r_in.at[0], me.to_core())
    rz = send(RD, RE, r_out.at[4], r_in.at[1], me.to_zl())

    def rotate_0():
        for k in (1, 2, 3):
            rx(k).start()

    def rotate_1():
        for k in (1, 2, 3):
            rx(k).wait_recv()

        @pl.loop(0, NQ)
        def _(q):
            total = x_sign(me, me.x) * RA[q]
            for k in (1, 2, 3):
                total = total + x_sign(me, me.at_x(-k)) * RX[k - 1, q]
            RB[q] = total

        rc.start()

    def rotate_2():
        rc.wait_recv()

        @pl.loop(0, NQ)
        def _(q):
            RD[q] = RC[q] + sign_of(me.core) * RB[q]

        rz.start()

    def rotate_3():
        rz.wait_recv()

        @pl.loop(0, NQ)
        def _(q):
            DH[q] = (RE[q] + sign_of(me.zl) * RD[q]) * (1.0 / math.sqrt(BLK * 16))

    @pl.loop(0, NP + LAG_E)
    def _(i):
        @pl.when(i == 1)
        def _():
            gather_x(1)

        @pl.when(i == 3)
        def _():
            gather_core(1)

        @pl.when(i == ROT_0)
        def _():
            rotate_0()

        @pl.when(i == ROT_0 + 6)
        def _():
            rotate_1()

        @pl.when(i == ROT_0 + 8)
        def _():
            rotate_2()

        for stage, lag in ((stage_a, 0), (stage_b, LAG_B), (stage_c, LAG_C), (stage_d, LAG_D), (stage_e, LAG_E)):

            @pl.when((i >= lag) & (i < NP + lag))
            def _(stage=stage, lag=lag):
                stage(i - lag)

    rotate_3()
    for s in (0, 1):
        sent = X.at[s, pl.ds(0, 15)]
        send(sent, sent, gs.at[s], gz.at[s], me.to_zl()).wait_send()
    send(s1s, s1r, s1_out, s1_in.at[0, 0], me.dp_y(1)).wait_send()
    send(s2s, s2r, s2_out, s2_in.at[0, 0], me.dp_y(1)).wait_send()
    send(z1s, z1r, z1_out, z1_in.at[0, 0], me.dp_z(1)).wait_send()
    send(z2s, z2r, z2_out, z2_in.at[0, 0], me.dp_z(1)).wait_send()
    for k in (1, 2, 3):
        rx(k).wait_send()
    rc.wait_send()
    rz.wait_send()


def reduce_phase(tokens, cotangent, w_gate, w_up, w_down):
    whole = pl.BlockSpec(memory_space=pltpu.VMEM)
    any_space = pl.BlockSpec(memory_space=pl.ANY)
    dma = pltpu.SemaphoreType.DMA
    rot = pltpu.VMEM((NQ, 48, 256), F32)
    return pl.pallas_call(
        reduce_kernel,
        out_shape=(
            jax.ShapeDtypeStruct((2, 16, 48, 512), BF),
            jax.ShapeDtypeStruct((2 * NQ, 48, 256), F32),
            jax.ShapeDtypeStruct((NQ, 48, 256), F32),
        ),
        in_specs=[whole, whole, any_space, any_space, any_space, whole],
        out_specs=(whole, whole, whole),
        scratch_shapes=[
            pltpu.VMEM((NP, 512, 256), BF),
            pltpu.VMEM((1792, 512), BF),
            pltpu.VMEM((NP, 2, 192, 128), BF),
            pltpu.VMEM((NP, 2, 192, 128), BF),
            pltpu.VMEM((NP, 2, 2, 192, 128), BF),
            pltpu.VMEM((NP, 2, 2, 192, 128), BF),
            pltpu.VMEM((NP, 2, 4, 48, 128), F32),
            pltpu.VMEM((NP, 2, 48, 128), BF),
            pltpu.VMEM((NP, 2, 48, 128), BF),
            pltpu.VMEM((NP, 2, 2, 48, 128), BF),
            pltpu.VMEM((NP, 2, 2, 48, 128), BF),
            rot, pltpu.VMEM((3, NQ, 48, 256), F32), rot, rot, rot, rot,
            dma((15,)), dma((2,)), dma((2, 2, 3)), dma((2, 8)), dma((2,)),
            dma, dma((NP, 2)), dma, dma((NP, 2)), dma, dma((NP, 2)), dma, dma((NP, 2)),
            dma((3,)), dma((2,)), dma((5,)),
        ],
        compiler_params=pltpu.CompilerParams(
            collective_id=0, has_side_effects=True, vmem_limit_bytes=56 * 1024 * 1024
        ),
        name="reduce_phase",
    )(tokens, cotangent, w_gate, w_up, w_down, sylvester(BLK, BF))


def spread_kernel(
    gu, dh, wg, wu, had,
    Gg, Gu, Gr, DT,
    WG, WU, HID, HX, RB, RC, RD, RE, PT, PR, XR, SZ, ZR,
    load_sem, out, zf, zhf, yf, yhf, hx_in, r_in, r_out, core_in, x_in, zl_in, t_out, x_out,
):
    me = Place()
    loads = [pltpu.make_async_copy(wg, WG, load_sem.at[0]), pltpu.make_async_copy(wu, WU, load_sem.at[1])]
    for load in loads:
        load.start()
    me.meet()
    grads = (Gg, Gu, Gr)

    def block(y, z):
        return y * 4 + z

    def part(s, index, half=None):
        if half is None:
            return grads[s].at[index]
        return grads[s].at[index, :, pl.ds(896 * half, 896)]

    def z_full(s, way, index):
        return send(part(s, index), part(s, index), out.at[s], zf.at[s, way], me.dp_z(1 - 2 * way))

    def z_half(s, way, index):
        ref = part(s, index, way)
        return send(ref, ref, out.at[s], zhf.at[s, way], me.dp_z(1 - 2 * way))

    def y_full(s, way, r, index):
        return send(part(s, index), part(s, index), out.at[s], yf.at[s, way, r], me.dp_y(1 - 2 * way))

    def y_half(s, way, r, index):
        ref = part(s, index, way)
        return send(ref, ref, out.at[s], yhf.at[s, way, r], me.dp_y(1 - 2 * way))

    def along_y(s, r):
        for way in (0, 1):
            y_full(s, way, r, block(me.y, me.at_z(r))).start()

    def own_out(s):
        for way in (0, 1):
            z_full(s, way, me.dp).start()
        along_y(s, 0)

    def z_came(s):
        for way, r in ((0, -1), (1, 1)):
            index = block(me.y, me.at_z(r))
            z_full(s, way, index).wait_recv()
            z_half(s, way, index).start()
            along_y(s, r % 4)

    def z_done(s):
        for way in (0, 1):
            z_half(s, way, block(me.y, me.at_z(2))).wait_recv()
        along_y(s, 2)

    def y_came(s, r):
        for way in (0, 1):
            index = block(me.at_y(2 * way - 1), me.at_z(r))
            y_full(s, way, r, index).wait_recv()
            y_half(s, way, r, index).start()

    def y_done(s, r):
        for way in (0, 1):
            y_half(s, way, r, block(me.at_y(2), me.at_z(r))).wait_recv()

    def columns(q):
        return slice(256 * q, 256 * q + 256)

    for q in range(NQ):
        gate, up, d_hidden = gu[q], gu[NQ + q], dh[q]
        sigma = jax.nn.sigmoid(gate)
        Gg[me.dp, :, columns(q)] = (d_hidden * up * sigma * (1.0 + gate * (1.0 - sigma))).astype(BF)
    own_out(0)
    for q in range(NQ):
        gate, up, d_hidden = gu[q], gu[NQ + q], dh[q]
        silu_gate = gate * jax.nn.sigmoid(gate)
        HID[:, columns(q)] = (silu_gate * up).astype(BF)
        Gu[me.dp, :, columns(q)] = (d_hidden * silu_gate).astype(BF)

    def hx(k):
        return send(HID, HX.at[k - 1], r_out.at[k - 1], hx_in.at[k - 1], me.to_x(k))

    rc = send(RB, RC, r_out.at[3], r_in.at[0], me.to_core())
    rz = send(RD, RE, r_out.at[4], r_in.at[1], me.to_zl())
    for k in (1, 2, 3):
        hx(k).start()
    own_out(1)
    z_came(0)
    for k in (1, 2, 3):
        hx(k).wait_recv()
    for q in range(NQ):
        total = x_sign(me, me.x) * HID[:, columns(q)].astype(F32)
        for k in (1, 2, 3):
            total = total + x_sign(me, me.at_x(-k)) * HX[k - 1, :, columns(q)].astype(F32)
        RB[q] = inner_hadamard(total, had[...])
    rc.start()
    z_came(1)
    z_done(0)
    rc.wait_recv()
    for q in range(NQ):
        RD[q] = RC[q] + sign_of(me.core) * RB[q]
    rz.start()
    y_came(0, 0)
    z_done(1)
    y_came(1, 0)
    rz.wait_recv()
    for q in range(NQ):
        total = (RE[q] + sign_of(me.zl) * RD[q]) * (1.0 / math.sqrt(BLK * 16))
        Gr[me.dp, :, columns(q)] = total.astype(BF)
    own_out(2)
    for r in (3, 1, 2):
        y_came(0, r)
    z_came(2)
    y_came(1, 3)
    z_done(2)
    for r in (1, 2):
        y_came(1, r)
    for load in loads:
        load.wait()
    for s in (0, 1):
        for r in (0, 3, 1, 2):
            y_done(s, r)

    weights = (((1,), (1,)), ((), ()))
    to_core = send(PT.at[1 - me.core], PR, t_out.at[0], core_in, me.to_core())

    def term(core, half):
        rows = [
            jnp.concatenate([G[2 * j + core] for j in range(4 * half, 4 * half + 4)], axis=0) for G in (Gg, Gu)
        ]
        total = lax.dot_general(rows[0], WG[...], weights, preferred_element_type=F32)
        total = total + lax.dot_general(rows[1], WU[...], weights, preferred_element_type=F32)
        PT[core, pl.ds(4 * half, 4)] = total.reshape(4, 48, 512)

    for half in (0, 1):
        term(1 - me.core, half)
    to_core.start()
    for half in (0, 1):
        term(me.core, half)
    y_came(2, 0)
    to_core.wait_recv()
    for j in range(8):
        PR[j] = PR[j] + PT[me.core, j]

    def x_term(k, zl):
        return send(
            PR.at[4 * zl + me.at_x(k)], XR.at[k - 1, zl], x_out.at[k - 1, zl], x_in.at[k - 1, zl], me.to_x(k)
        )

    for k in (1, 2, 3):
        for zl in (0, 1):
            x_term(k, zl).start()
    y_came(2, 3)
    for k in (1, 2, 3):
        for zl in (0, 1):
            x_term(k, zl).wait_recv()
    for zl in (0, 1):
        SZ[zl] = PR[4 * zl + me.x] + XR[0, zl] + XR[1, zl] + XR[2, zl]
    to_zl = send(SZ.at[1 - me.zl], ZR, t_out.at[1], zl_in, me.to_zl())
    to_zl.start()
    y_came(2, 1)
    to_zl.wait_recv()
    DT[...] = (SZ[me.zl] + ZR[...]).astype(BF)
    y_came(2, 2)
    for r in (0, 3, 1, 2):
        y_done(2, r)
    for s in (0, 1, 2):
        sent = grads[s].at[pl.ds(0, 15)]
        send(sent, sent, out.at[s], zf.at[s, 0], me.dp_y(1)).wait_send()
    for k in (1, 2, 3):
        hx(k).wait_send()
        for zl in (0, 1):
            x_term(k, zl).wait_send()
    for copy in (rc, rz, to_core, to_zl):
        copy.wait_send()


def spread_phase(GU, DH, w_gate, w_up):
    whole = pl.BlockSpec(memory_space=pltpu.VMEM)
    any_space = pl.BlockSpec(memory_space=pl.ANY)
    dma = pltpu.SemaphoreType.DMA
    rot = pltpu.VMEM((NQ, 48, 256), F32)
    full = jax.ShapeDtypeStruct((16, 48, 1792), BF)
    return pl.pallas_call(
        spread_kernel,
        out_shape=(full, full, full, jax.ShapeDtypeStruct((48, 512), BF)),
        in_specs=[whole, whole, any_space, any_space, whole],
        out_specs=(whole,) * 4,
        scratch_shapes=[
            pltpu.VMEM((512, 1792), BF),
            pltpu.VMEM((512, 1792), BF),
            pltpu.VMEM((48, 1792), BF),
            pltpu.VMEM((3, 48, 1792), BF),
            rot, rot, rot, rot,
            pltpu.VMEM((2, 8, 48, 512), F32),
            pltpu.VMEM((8, 48, 512), F32),
            pltpu.VMEM((3, 2, 48, 512), F32),
            pltpu.VMEM((2, 48, 512), F32),
            pltpu.VMEM((48, 512), F32),
            dma((2,)), dma((3,)), dma((3, 2)), dma((3, 2)), dma((3, 2, 4)), dma((3, 2, 4)),
            dma((3,)), dma((2,)), dma((5,)), dma, dma((3, 2)), dma, dma((2,)), dma((3, 2)),
        ],
        compiler_params=pltpu.CompilerParams(
            collective_id=1, has_side_effects=True, vmem_limit_bytes=56 * 1024 * 1024
        ),
        name="spread_phase",
    )(GU, DH, w_gate, w_up, sylvester(BLK, BF))


def per_device(tokens, w_gate, w_up, w_down, cotangent):
    X, GU, DH = reduce_phase(tokens, cotangent, w_gate, w_up, w_down)
    all_cotangent, all_tokens = X[0].reshape(768, 512), X[1].reshape(768, 512)
    grads_gate, grads_up, rotated, d_tokens = spread_phase(GU, DH, w_gate, w_up)
    contract_rows = (((0,), (0,)), ((), ()))

    def product(left, right):
        return lax.dot_general(left, right, contract_rows, preferred_element_type=F32).astype(BF)

    d_gate = product(all_tokens, grads_gate.reshape(768, 1792))
    d_up = product(all_tokens, grads_up.reshape(768, 1792))
    d_down = product(rotated.reshape(768, 1792), all_cotangent)
    return (d_tokens, d_gate, d_up, d_down)


def solution(mesh):
    return jax.shard_map(
        per_device,
        mesh=mesh,
        in_specs=(
            P("tensor", "dp"),
            P("dp", "tensor"),
            P("dp", "tensor"),
            P("tensor", "dp"),
            P("tensor", "dp"),
        ),
        out_specs=(P("tensor", "dp"), P("dp", "tensor"), P("dp", "tensor"), P("tensor", "dp")),
        check_vma=False,
    )
```

```python
import functools
import math

import jax
import jax.numpy as jnp
from jax import lax
from jax.experimental import pallas as pl
from jax.experimental.pallas import tpu as pltpu
from jax.sharding import PartitionSpec as P

BLK = 128
BF = jnp.bfloat16
F32 = jnp.float32
MESH = pl.DeviceIdType.MESH
NQ = 7
NP = 3 * NQ
LAG_B, LAG_C, LAG_D, LAG_E = 1, 3, 4, 5
ROT_X, ROT_CORE, ROT_ZL, ROT_END = 12, 17, 18, 21
GRADS = 21
HID_X, HID_CORE, HID_ZL, HID_END = 27, 29, 30, 32
SPREAD = (0, 1, 2, 4, 6)
SUM_X, SUM_ZL = 34, 37
STEPS = HID_END + SPREAD[4] + NQ


def reduce_flag(p):
    return jnp.where(lax.rem(p, 4) == 3, 1, 0)


def grads_flag(q):
    return jnp.where(lax.rem(q, 3) == 2, 1, 0)


def rotated_flag(q):
    return jnp.where(q == 3, 1, 0)


def sylvester(order, dtype=jnp.float32):
    positions = jnp.arange(order, dtype=jnp.int32)
    row_ids = positions[:, None]
    col_ids = positions[None, :]
    signs = jnp.ones((order, order), jnp.float32)
    for power in range(order.bit_length() - 1):
        both = (row_ids >> power & 1) * (col_ids >> power & 1)
        signs = signs * (1 - 2 * both).astype(jnp.float32)
    return signs.astype(dtype)


def around(position, step):
    return lax.rem(position + step + 4, 4)


class Place:
    def __init__(self):
        self.dp = lax.axis_index("dp")
        self.t = lax.axis_index("tensor")
        self.y, self.zh = lax.div(self.dp, 4), lax.rem(self.dp, 4)
        self.zl = lax.div(self.t, 8)
        self.x = lax.rem(lax.div(self.t, 2), 4)
        self.core = lax.rem(self.t, 2)

    def axes(self, flag):
        return self.y + flag * (self.zh - self.y), self.zh + flag * (self.y - self.zh)

    def dp_of(self, flag, first, second):
        return {"dp": (4 - 3 * flag) * first + (1 + 3 * flag) * second, "tensor": self.t}

    def at_x(self, step):
        return lax.rem(self.x + step + 4, 4)

    def slot(self, zl, x, core):
        return zl * 8 + x * 2 + core

    def to_x(self, step):
        return {"dp": self.dp, "tensor": self.slot(self.zl, self.at_x(step), self.core)}

    def to_core(self):
        return {"dp": self.dp, "tensor": self.slot(self.zl, self.x, 1 - self.core)}

    def to_zl(self):
        return {"dp": self.dp, "tensor": self.slot(1 - self.zl, self.x, self.core)}

    def meet(self):
        peers = []
        for step in (1, -1):
            peers.append(self.dp_of(0, around(self.y, step), self.zh))
            peers.append(self.dp_of(0, self.y, around(self.zh, step)))
        peers += [self.to_x(k) for k in (1, 2, 3)] + [self.to_core(), self.to_zl()]
        barrier = pltpu.get_barrier_semaphore()
        for peer in peers:
            pl.semaphore_signal(barrier, inc=1, device_id=peer, device_id_type=MESH)
        pl.semaphore_wait(barrier, len(peers))


def send(src, dst, send_sem, recv_sem, to):
    return pltpu.make_async_remote_copy(
        src_ref=src, dst_ref=dst, send_sem=send_sem, recv_sem=recv_sem, device_id=to, device_id_type=MESH
    )


def sign_of(bit):
    return (1 - 2 * bit).astype(F32)


def x_sign(place, other):
    both = lax.rem(place.x, 2) * lax.rem(other, 2) + lax.div(place.x, 2) * lax.div(other, 2)
    return sign_of(lax.rem(both, 2))


def inner_hadamard(value, had):
    parts = []
    for start in range(0, value.shape[1], BLK):
        block = value[:, start : start + BLK]
        high = block.astype(BF)
        low = (block - high.astype(F32)).astype(BF)
        parts.append(
            jnp.dot(high, had, preferred_element_type=F32) + jnp.dot(low, had, preferred_element_type=F32)
        )
    return jnp.concatenate(parts, axis=1)


def layer_kernel(
    tok, cot, wg, wu, wd, had,
    DG, DU, DD, DT,
    X, XT, W, WD, s1s, s1r, s2s, s2r, T, z1s, z1r, z2s, z2r, GU, DH,
    RA, RX, RB, RC, RD, RE, HID, HX, HB, HC, HD, HE, AG, AR, OW, OD, PT, PR, XR, SZ, ZR,
    load_sem, gz, gx, gc, gs, s1_out, s1_in, s2_out, s2_in, z1_out, z1_in, z2_out, z2_in,
    rx_in, r_in, r_out, hx_in, h_in, h_out, ag_out, a2f, a2h, a1f, a1h, core_in, x_in, zl_in, t_out, x_out, o_sem,
):
    me = Place()
    loads = [pltpu.make_async_copy(wd, WD, load_sem.at[0])]
    for q in range(NQ):
        loads.append(pltpu.make_async_copy(wg.at[:, pl.ds(256 * q, 256)], W.at[NQ + 2 * q], load_sem.at[1 + q]))
        loads.append(pltpu.make_async_copy(wu.at[:, pl.ds(256 * q, 256)], W.at[NQ + 2 * q + 1], load_sem.at[1 + NQ + q]))
    for load in loads:
        load.start()
    me.meet()

    other = me.slot(1 - me.zl, me.x, me.core)

    def gather_own(s, own):
        X[s, me.t] = own[...]
        send(X.at[s, me.t], X.at[s, me.t], gs.at[s], gz.at[s], me.to_zl()).start()
        for k in (1, 2, 3):
            send(X.at[s, me.t], X.at[s, me.t], gs.at[s], gx.at[s, 0, k - 1], me.to_x(k)).start()

    def gather_zl(s):
        send(X.at[s, other], X.at[s, other], gs.at[s], gz.at[s], me.to_zl()).wait_recv()
        for k in (1, 2, 3):
            send(X.at[s, other], X.at[s, other], gs.at[s], gx.at[s, 1, k - 1], me.to_x(k)).start()

    def to_core(s, zl, x, n):
        block = X.at[s, me.slot(zl, x, me.core)]
        send(block, block, gs.at[s], gc.at[s, n], me.to_core()).start()

    def gather_x(s):
        to_core(s, me.zl, me.x, 0)
        to_core(s, 1 - me.zl, me.x, 4)
        for j, zl in ((0, me.zl), (1, 1 - me.zl)):
            for k in (1, 2, 3):
                came = me.at_x(-k)
                block = X.at[s, me.slot(zl, came, me.core)]
                send(block, block, gs.at[s], gx.at[s, j, k - 1], me.to_x(k)).wait_recv()
                to_core(s, zl, came, 4 * j + k)

    def gather_core(s):
        for j, zl in ((0, me.zl), (1, 1 - me.zl)):
            for k in range(4):
                block = X.at[s, me.slot(zl, me.at_x(-k), 1 - me.core)]
                send(block, block, gs.at[s], gc.at[s, 4 * j + k], me.to_core()).wait_recv()

    gather_own(0, cot)
    loads[0].wait()
    for q in range(3):
        W[q] = WD[pl.ds(256 * q, 256), :].T
    gather_zl(0)
    gather_own(1, tok)
    for q in range(3, NQ):
        W[q] = WD[pl.ds(256 * q, 256), :].T
    gather_zl(1)
    PT[...] = jnp.zeros_like(PT)
    gather_x(0)
    gather_core(0)
    for load in loads[1:]:
        load.wait()

    def partial(p, flag, first):
        s = jnp.where(p < NQ, 0, 1)
        rows = [X[s, (4 - 3 * flag) * first + (1 + 3 * flag) * j] for j in range(4)]
        return jnp.dot(jnp.concatenate(rows, axis=0), W[p], preferred_element_type=F32)

    def ring_1(p, way, src, dst, out, came):
        flag = reduce_flag(p)
        first, second = me.axes(flag)
        to = me.dp_of(flag, around(first, 1 - 2 * way), second)
        return send(src.at[p, way], dst.at[p, way], out, came.at[p, way], to)

    def ring_2(p, way, src, dst, out, came):
        flag = reduce_flag(p)
        first, second = me.axes(flag)
        to = me.dp_of(flag, first, around(second, 1 - 2 * way))
        return send(src.at[p, way], dst.at[p, way], out, came.at[p, way], to)

    def s1(p, way):
        return ring_1(p, way, s1s, s1r, s1_out, s1_in)

    def s2(p, way):
        return ring_1(p, way, s2s, s2r, s2_out, s2_in)

    def z1(p, way):
        return ring_2(p, way, z1s, z1r, z1_out, z1_in)

    def z2(p, way):
        return ring_2(p, way, z2s, z2r, z2_out, z2_in)

    def stage_a(p):
        flag = reduce_flag(p)
        far = partial(p, flag, around(me.axes(flag)[0], 2)).astype(BF)
        for way in (0, 1):
            s1s[p, way] = far[:, 128 * way : 128 * way + 128]
            s1(p, way).start()

    def stage_b(p):
        flag = reduce_flag(p)
        for way in (0, 1):
            near = partial(p, flag, around(me.axes(flag)[0], 1 - 2 * way))
            s1(p, way).wait_recv()
            for half in (0, 1):
                value = near[:, 128 * half : 128 * half + 128]
                if half == way:
                    value = value + s1r[p, way].astype(F32)
                s2s[p, way, half] = value.astype(BF)
            s2(p, way).start()

    def stage_c(p):
        flag = reduce_flag(p)
        first, second = me.axes(flag)
        own = partial(p, flag, first)
        s2(p, 0).wait_recv()
        s2(p, 1).wait_recv()
        for half in (0, 1):
            value = own[:, 128 * half : 128 * half + 128]
            value = value + s2r[p, 0, half].astype(F32) + s2r[p, 1, half].astype(F32)
            T[p, half] = value.reshape(4, 48, 128)
        for way in (0, 1):
            z1s[p, way] = T[p, way, around(second, 2)].astype(BF)
            z1(p, way).start()

    def stage_d(p):
        second = me.axes(reduce_flag(p))[1]
        for way in (0, 1):
            z1(p, way).wait_recv()
            for half in (0, 1):
                value = T[p, half, around(second, 1 - 2 * way)]
                if half == way:
                    value = value + z1r[p, way].astype(F32)
                z2s[p, way, half] = value.astype(BF)
            z2(p, way).start()

    def stage_e(p):
        second = me.axes(reduce_flag(p))[1]
        z2(p, 0).wait_recv()
        z2(p, 1).wait_recv()
        halves = [
            T[p, half, second] + z2r[p, 0, half].astype(F32) + z2r[p, 1, half].astype(F32) for half in (0, 1)
        ]
        total = jnp.concatenate(halves, axis=1)

        @pl.when(p < NQ)
        def _():
            RA[p] = inner_hadamard(total, had[...])

        @pl.when(p >= NQ)
        def _():
            GU[p - NQ] = total

    def outer(own, came, half_1, came_1, half_2, came_2, x_sem, in_sem, out_sem):
        def x_copy(k):
            return send(own, came.at[k - 1], out_sem.at[k - 1], x_sem.at[k - 1], me.to_x(k))

        core_copy = send(half_1, came_1, out_sem.at[3], in_sem.at[0], me.to_core())
        zl_copy = send(half_2, came_2, out_sem.at[4], in_sem.at[1], me.to_zl())

        def start():
            for k in (1, 2, 3):
                x_copy(k).start()

        def along_x(inner):
            for k in (1, 2, 3):
                x_copy(k).wait_recv()

            @pl.loop(0, NQ)
            def _(q):
                total = x_sign(me, me.x) * own[q].astype(F32)
                for k in (1, 2, 3):
                    total = total + x_sign(me, me.at_x(-k)) * came[k - 1, q].astype(F32)
                half_1[q] = inner(total)

            core_copy.start()

        def cores():
            core_copy.wait_recv()

            @pl.loop(0, NQ)
            def _(q):
                half_2[q] = came_1[q] + sign_of(me.core) * half_1[q]

            zl_copy.start()

        def along_zl(store):
            zl_copy.wait_recv()

            @pl.loop(0, NQ)
            def _(q):
                store(q, (came_2[q] + sign_of(me.zl) * half_2[q]) * (1.0 / math.sqrt(BLK * 16)))

        def finish():
            for k in (1, 2, 3):
                x_copy(k).wait_send()
            core_copy.wait_send()
            zl_copy.wait_send()

        return start, along_x, cores, along_zl, finish

    rot = outer(RA, RX, RB, RC, RD, RE, rx_in, r_in, r_out)
    hid = outer(HID, HX, HB, HC, HD, HE, hx_in, h_in, h_out)

    def gathering(buf, row, flag_of):
        def place(u):
            flag = flag_of(u)
            return flag, *me.axes(flag)

        def second_copy(u, way, at, half=None):
            flag, first, second = place(u)
            part = slice(None) if half is None else half
            ref = buf.at[u, part, 4 * first + at]
            sem = (a2f if half is None else a2h).at[row + u, way]
            return send(ref, ref, ag_out.at[row // NQ], sem, me.dp_of(flag, first, around(second, 1 - 2 * way)))

        def first_copy(u, way, at, half=None):
            flag, first, second = place(u)
            part = slice(None) if half is None else half
            ref = buf.at[u, part, pl.ds(4 * at, 4)]
            sem = (a1f if half is None else a1h).at[row + u, way]
            return send(ref, ref, ag_out.at[row // NQ], sem, me.dp_of(flag, around(first, 1 - 2 * way), second))

        def begin(u):
            for way in (0, 1):
                second_copy(u, way, place(u)[2]).start()

        def pass_second(u):
            for way in (0, 1):
                at = around(place(u)[2], 2 * way - 1)
                second_copy(u, way, at).wait_recv()
                second_copy(u, way, at, way).start()

        def begin_first(u):
            for way in (0, 1):
                second_copy(u, way, around(place(u)[2], 2), way).wait_recv()
            for way in (0, 1):
                first_copy(u, way, place(u)[1]).start()

        def pass_first(u):
            for way in (0, 1):
                at = around(place(u)[1], 2 * way - 1)
                first_copy(u, way, at).wait_recv()
                first_copy(u, way, at, way).start()

        def complete(u):
            for way in (0, 1):
                first_copy(u, way, around(place(u)[1], 2), way).wait_recv()

        def finish():
            sent = buf.at[:, :, pl.ds(0, 15)]
            send(sent, sent, ag_out.at[row // NQ], a2f.at[0, 0], me.to_zl()).wait_send()

        return begin, pass_second, begin_first, pass_first, complete, finish

    def own_position(flag):
        first, second = me.axes(flag)
        return 4 * first + second

    def in_order(flag, block):
        halves = []
        for half in (0, 1):
            rows = [block(half, (4 - 3 * flag) * (d // 4) + (1 + 3 * flag) * (d % 4)) for d in range(16)]
            halves.append(jnp.concatenate(rows, axis=0))
        return jnp.concatenate(halves, axis=1)

    grads = gathering(AG, 0, grads_flag)
    turned = gathering(AR, NQ, rotated_flag)

    def grads_begin(q):
        gate, up, d_hidden = GU[2 * q], GU[2 * q + 1], DH[q]
        sigma = jax.nn.sigmoid(gate)
        silu_gate = gate * sigma
        HID[q] = (silu_gate * up).astype(BF)
        pair = (
            (d_hidden * up * sigma * (1.0 + gate * (1.0 - sigma))).astype(BF),
            (d_hidden * silu_gate).astype(BF),
        )
        at = own_position(grads_flag(q))
        for s in (0, 1):
            for half in (0, 1):
                AG[q, half, at, s] = pair[s][:, 128 * half : 128 * half + 128]
        grads[0](q)

    def out_grad(q, s):
        to = (DG, DU)[s].at[:, pl.ds(pl.multiple_of(256 * q, 256), 256)]
        return pltpu.make_async_copy(OW.at[q, s], to, o_sem.at[q, s])

    def out_down(q):
        to = DD.at[pl.ds(pl.multiple_of(256 * q, 256), 256)]
        return pltpu.make_async_copy(OD.at[q], to, o_sem.at[q, 2])

    def grads_end(q):
        grads[4](q)
        flag = grads_flag(q)
        total = None
        for s in (0, 1):
            value = in_order(flag, lambda half, at: AG[q, half, at, s])
            OW[q, s] = jnp.dot(XT[...], value, preferred_element_type=F32).astype(BF)
            out_grad(q, s).start()
            term = lax.dot_general(
                value, W[NQ + 2 * q + s], (((1,), (1,)), ((), ())), preferred_element_type=F32
            )
            total = term if total is None else total + term
        for n in range(16):
            PT[n % 2, n // 2] += total[48 * n : 48 * n + 48]

    def rotated_store(q, value):
        at = own_position(rotated_flag(q))
        for half in (0, 1):
            AR[q, half, at] = value[:, 128 * half : 128 * half + 128].astype(BF)
        turned[0](q)

    def rotated_end(q):
        turned[4](q)
        value = in_order(rotated_flag(q), lambda half, at: AR[q, half, at])
        OD[q] = jnp.dot(value.T, X[0].reshape(768, 512), preferred_element_type=F32).astype(BF)
        out_down(q).start()

    sum_core = send(PT.at[1 - me.core], PR, t_out.at[0], core_in, me.to_core())
    sum_zl = send(SZ.at[1 - me.zl], ZR, t_out.at[1], zl_in, me.to_zl())

    def sum_x(k, zl):
        return send(
            PR.at[4 * zl + me.at_x(k)], XR.at[k - 1, zl], x_out.at[k - 1, zl], x_in.at[k - 1, zl], me.to_x(k)
        )

    def sum_1():
        sum_core.wait_recv()
        for j in range(8):
            PR[j] = PR[j] + PT[me.core, j]
        for k in (1, 2, 3):
            for zl in (0, 1):
                sum_x(k, zl).start()

    def sum_2():
        for k in (1, 2, 3):
            for zl in (0, 1):
                sum_x(k, zl).wait_recv()
        for zl in (0, 1):
            SZ[zl] = PR[4 * zl + me.x] + XR[0, zl] + XR[1, zl] + XR[2, zl]
        sum_zl.start()

    def store_d_hidden(q, value):
        DH[q] = value

    at_step = {
        1: lambda: gather_x(1),
        3: lambda: gather_core(1),
        ROT_X: rot[0],
        ROT_CORE: lambda: rot[1](lambda value: value),
        ROT_ZL: rot[2],
        ROT_END: lambda: rot[3](store_d_hidden),
        HID_CORE: lambda: hid[1](lambda value: inner_hadamard(value, had[...])),
        HID_ZL: hid[2],
        HID_END: lambda: hid[3](rotated_store),
        SUM_X: sum_1,
        SUM_ZL: sum_2,
    }
    stages = [(stage_a, 0, NP), (stage_b, LAG_B, NP), (stage_c, LAG_C, NP), (stage_d, LAG_D, NP), (stage_e, LAG_E, NP)]
    stages += [(grads_begin, GRADS, NQ)]
    stages += [(grads[n], GRADS + SPREAD[n], NQ) for n in (1, 2, 3)]
    stages += [(turned[n], HID_END + SPREAD[n], NQ) for n in (1, 2, 3)]
    stages += [(grads_end, GRADS + SPREAD[4], NQ), (rotated_end, HID_END + SPREAD[4], NQ)]

    @pl.loop(0, STEPS)
    def _(i):
        for step, work in at_step.items():
            pl.when(i == step)(work)
        for stage, first, count in stages:

            @pl.when((i >= first) & (i < first + count))
            def _(stage=stage, first=first):
                stage(i - first)

        @pl.when(i == 5)
        def _():
            XT[...] = X[1].reshape(768, 512).T

        pl.when(i == HID_X)(hid[0])
        pl.when(i == GRADS + SPREAD[4] + NQ - 1)(sum_core.start)

    sum_zl.wait_recv()
    DT[...] = (SZ[me.zl] + ZR[...]).astype(BF)
    for q in range(NQ):
        for s in (0, 1):
            out_grad(q, s).wait()
        out_down(q).wait()
    for s in (0, 1):
        sent = X.at[s, pl.ds(0, 15)]
        send(sent, sent, gs.at[s], gz.at[s], me.to_zl()).wait_send()
    for src, dst, out in ((s1s, s1r, s1_out), (s2s, s2r, s2_out), (z1s, z1r, z1_out), (z2s, z2r, z2_out)):
        send(src, dst, out, gz.at[0], me.to_zl()).wait_send()
    rot[4]()
    hid[4]()
    grads[5]()
    turned[5]()
    sum_core.wait_send()
    sum_zl.wait_send()
    for k in (1, 2, 3):
        for zl in (0, 1):
            sum_x(k, zl).wait_send()


def per_device(tokens, w_gate, w_up, w_down, cotangent):
    whole = pl.BlockSpec(memory_space=pltpu.VMEM)
    any_space = pl.BlockSpec(memory_space=pl.ANY)
    dma = pltpu.SemaphoreType.DMA
    part, part_bf = pltpu.VMEM((NQ, 48, 256), F32), pltpu.VMEM((NQ, 48, 256), BF)
    d_gate, d_up, d_down, d_tokens = pl.pallas_call(
        layer_kernel,
        out_shape=(
            jax.ShapeDtypeStruct((512, 1792), BF),
            jax.ShapeDtypeStruct((512, 1792), BF),
            jax.ShapeDtypeStruct((1792, 512), BF),
            jax.ShapeDtypeStruct((48, 512), BF),
        ),
        in_specs=[whole, whole, any_space, any_space, any_space, whole],
        out_specs=(any_space, any_space, any_space, whole),
        scratch_shapes=[
            pltpu.VMEM((2, 16, 48, 512), BF),
            pltpu.VMEM((512, 768), BF),
            pltpu.VMEM((NP, 512, 256), BF),
            pltpu.VMEM((1792, 512), BF),
            pltpu.VMEM((NP, 2, 192, 128), BF),
            pltpu.VMEM((NP, 2, 192, 128), BF),
            pltpu.VMEM((NP, 2, 2, 192, 128), BF),
            pltpu.VMEM((NP, 2, 2, 192, 128), BF),
            pltpu.VMEM((NP, 2, 4, 48, 128), F32),
            pltpu.VMEM((NP, 2, 48, 128), BF),
            pltpu.VMEM((NP, 2, 48, 128), BF),
            pltpu.VMEM((NP, 2, 2, 48, 128), BF),
            pltpu.VMEM((NP, 2, 2, 48, 128), BF),
            pltpu.VMEM((2 * NQ, 48, 256), F32),
            part,
            part, pltpu.VMEM((3, NQ, 48, 256), F32), part, part, part, part,
            part_bf, pltpu.VMEM((3, NQ, 48, 256), BF), part, part, part, part,
            pltpu.VMEM((NQ, 2, 16, 2, 48, 128), BF),
            pltpu.VMEM((NQ, 2, 16, 48, 128), BF),
            pltpu.VMEM((NQ, 2, 512, 256), BF),
            pltpu.VMEM((NQ, 256, 512), BF),
            pltpu.VMEM((2, 8, 48, 512), F32),
            pltpu.VMEM((8, 48, 512), F32),
            pltpu.VMEM((3, 2, 48, 512), F32),
            pltpu.VMEM((2, 48, 512), F32),
            pltpu.VMEM((48, 512), F32),
            dma((15,)), dma((2,)), dma((2, 2, 3)), dma((2, 8)), dma((2,)),
            dma, dma((NP, 2)), dma, dma((NP, 2)), dma, dma((NP, 2)), dma, dma((NP, 2)),
            dma((3,)), dma((2,)), dma((5,)), dma((3,)), dma((2,)), dma((5,)),
            dma((2,)), dma((2 * NQ, 2)), dma((2 * NQ, 2)), dma((2 * NQ, 2)), dma((2 * NQ, 2)),
            dma, dma((3, 2)), dma, dma((2,)), dma((3, 2)), dma((NQ, 3)),
        ],
        compiler_params=pltpu.CompilerParams(
            collective_id=0, has_side_effects=True, vmem_limit_bytes=60 * 1024 * 1024
        ),
        name="layer_backward",
    )(tokens, cotangent, w_gate, w_up, w_down, sylvester(BLK, BF))
    return (d_tokens, d_gate, d_up, d_down)


def solution(mesh):
    return jax.shard_map(
        per_device,
        mesh=mesh,
        in_specs=(
            P("tensor", "dp"),
            P("dp", "tensor"),
            P("dp", "tensor"),
            P("tensor", "dp"),
            P("tensor", "dp"),
        ),
        out_specs=(P("tensor", "dp"), P("dp", "tensor"), P("dp", "tensor"), P("tensor", "dp")),
        check_vma=False,
    )
```

```python
import functools
import math

import jax
import jax.numpy as jnp
from jax import lax
from jax.experimental import pallas as pl
from jax.experimental.pallas import tpu as pltpu
from jax.sharding import PartitionSpec as P

BLK = 128
BF = jnp.bfloat16
F32 = jnp.float32
MESH = pl.DeviceIdType.MESH
NQ = 7
NP = 3 * NQ
LAG_B, LAG_C, LAG_D, LAG_E = 3, 6, 9, 12
ROT_X, ROT_CORE, ROT_ZL, ROT_END = 19, 24, 26, 29
GRADS = 29
HID_X, HID_CORE, HID_ZL, HID_END = 35, 38, 41, 44
SPREAD = (0, 4, 8, 14, 18)
SUM_X, SUM_ZL = 54, 58
STEPS = HID_END + SPREAD[4] + NQ


def reduce_flag(p):
    return jnp.where(lax.rem(p, 4) == 3, 1, 0)


def grads_flag(q):
    return jnp.where(lax.rem(q, 3) == 2, 1, 0)


def rotated_flag(q):
    return jnp.where(q == 3, 1, 0)


def sylvester(order, dtype=jnp.float32):
    positions = jnp.arange(order, dtype=jnp.int32)
    row_ids = positions[:, None]
    col_ids = positions[None, :]
    signs = jnp.ones((order, order), jnp.float32)
    for power in range(order.bit_length() - 1):
        both = (row_ids >> power & 1) * (col_ids >> power & 1)
        signs = signs * (1 - 2 * both).astype(jnp.float32)
    return signs.astype(dtype)


def around(position, step):
    return lax.rem(position + step + 4, 4)


class Place:
    def __init__(self):
        self.dp = lax.axis_index("dp")
        self.t = lax.axis_index("tensor")
        self.y, self.zh = lax.div(self.dp, 4), lax.rem(self.dp, 4)
        self.zl = lax.div(self.t, 8)
        self.x = lax.rem(lax.div(self.t, 2), 4)
        self.core = lax.rem(self.t, 2)

    def axes(self, flag):
        return self.y + flag * (self.zh - self.y), self.zh + flag * (self.y - self.zh)

    def dp_of(self, flag, first, second):
        return {"dp": (4 - 3 * flag) * first + (1 + 3 * flag) * second, "tensor": self.t}

    def at_x(self, step):
        return lax.rem(self.x + step + 4, 4)

    def slot(self, zl, x, core):
        return zl * 8 + x * 2 + core

    def to_x(self, step):
        return {"dp": self.dp, "tensor": self.slot(self.zl, self.at_x(step), self.core)}

    def to_core(self):
        return {"dp": self.dp, "tensor": self.slot(self.zl, self.x, 1 - self.core)}

    def to_zl(self):
        return {"dp": self.dp, "tensor": self.slot(1 - self.zl, self.x, self.core)}

    def meet(self):
        peers = []
        for step in (1, -1):
            peers.append(self.dp_of(0, around(self.y, step), self.zh))
            peers.append(self.dp_of(0, self.y, around(self.zh, step)))
        peers += [self.to_x(k) for k in (1, 2, 3)] + [self.to_core(), self.to_zl()]
        barrier = pltpu.get_barrier_semaphore()
        for peer in peers:
            pl.semaphore_signal(barrier, inc=1, device_id=peer, device_id_type=MESH)
        pl.semaphore_wait(barrier, len(peers))


def send(src, dst, send_sem, recv_sem, to):
    return pltpu.make_async_remote_copy(
        src_ref=src, dst_ref=dst, send_sem=send_sem, recv_sem=recv_sem, device_id=to, device_id_type=MESH
    )


def sign_of(bit):
    return (1 - 2 * bit).astype(F32)


def x_sign(place, other):
    both = lax.rem(place.x, 2) * lax.rem(other, 2) + lax.div(place.x, 2) * lax.div(other, 2)
    return sign_of(lax.rem(both, 2))


def inner_hadamard(value, had):
    parts = []
    for start in range(0, value.shape[1], BLK):
        block = value[:, start : start + BLK]
        high = block.astype(BF)
        low = (block - high.astype(F32)).astype(BF)
        parts.append(
            jnp.dot(high, had, preferred_element_type=F32) + jnp.dot(low, had, preferred_element_type=F32)
        )
    return jnp.concatenate(parts, axis=1)


def layer_kernel(
    tok, cot, wg, wu, wd, had,
    DG, DU, DD, DT,
    X, XT, W, WD, s1s, s1r, s2s, s2r, T, z1s, z1r, z2s, z2r, GU, DH,
    RA, RX, RB, RC, RD, RE, HID, HX, HB, HC, HD, HE, AG, AR, OW, OD, PT, PR, XR, SZ, ZR,
    load_sem, gz, gx, gc, gs, s1_out, s1_in, s2_out, s2_in, z1_out, z1_in, z2_out, z2_in,
    rx_in, r_in, r_out, hx_in, h_in, h_out, ag_out, a2f, a2h, a1f, a1h, core_in, x_in, zl_in, t_out, x_out, o_sem,
):
    me = Place()
    loads = [pltpu.make_async_copy(wd, WD, load_sem.at[0])]
    for q in range(NQ):
        loads.append(pltpu.make_async_copy(wg.at[:, pl.ds(256 * q, 256)], W.at[NQ + 2 * q], load_sem.at[1 + q]))
        loads.append(pltpu.make_async_copy(wu.at[:, pl.ds(256 * q, 256)], W.at[NQ + 2 * q + 1], load_sem.at[1 + NQ + q]))
    for load in loads:
        load.start()
    me.meet()

    other = me.slot(1 - me.zl, me.x, me.core)

    def gather_own(s, own):
        X[s, me.t] = own[...]
        send(X.at[s, me.t], X.at[s, me.t], gs.at[s], gz.at[s], me.to_zl()).start()
        for k in (1, 2, 3):
            send(X.at[s, me.t], X.at[s, me.t], gs.at[s], gx.at[s, 0, k - 1], me.to_x(k)).start()

    def gather_zl(s):
        send(X.at[s, other], X.at[s, other], gs.at[s], gz.at[s], me.to_zl()).wait_recv()
        for k in (1, 2, 3):
            send(X.at[s, other], X.at[s, other], gs.at[s], gx.at[s, 1, k - 1], me.to_x(k)).start()

    def to_core(s, zl, x, n):
        block = X.at[s, me.slot(zl, x, me.core)]
        send(block, block, gs.at[s], gc.at[s, n], me.to_core()).start()

    def gather_x(s):
        to_core(s, me.zl, me.x, 0)
        to_core(s, 1 - me.zl, me.x, 4)
        for j, zl in ((0, me.zl), (1, 1 - me.zl)):
            for k in (1, 2, 3):
                came = me.at_x(-k)
                block = X.at[s, me.slot(zl, came, me.core)]
                send(block, block, gs.at[s], gx.at[s, j, k - 1], me.to_x(k)).wait_recv()
                to_core(s, zl, came, 4 * j + k)

    def gather_core(s):
        for j, zl in ((0, me.zl), (1, 1 - me.zl)):
            for k in range(4):
                block = X.at[s, me.slot(zl, me.at_x(-k), 1 - me.core)]
                send(block, block, gs.at[s], gc.at[s, 4 * j + k], me.to_core()).wait_recv()

    gather_own(0, cot)
    loads[0].wait()
    for q in range(3):
        W[q] = WD[pl.ds(256 * q, 256), :].T
    gather_zl(0)
    gather_own(1, tok)
    for q in range(3, NQ):
        W[q] = WD[pl.ds(256 * q, 256), :].T
    gather_zl(1)
    PT[...] = jnp.zeros_like(PT)
    gather_x(0)
    gather_core(0)
    for load in loads[1:]:
        load.wait()

    def partial(p, flag, first):
        s = jnp.where(p < NQ, 0, 1)
        rows = [X[s, (4 - 3 * flag) * first + (1 + 3 * flag) * j] for j in range(4)]
        return jnp.dot(jnp.concatenate(rows, axis=0), W[p], preferred_element_type=F32)

    def ring_1(p, way, src, dst, out, came):
        flag = reduce_flag(p)
        first, second = me.axes(flag)
        to = me.dp_of(flag, around(first, 1 - 2 * way), second)
        return send(src.at[p, way], dst.at[p, way], out, came.at[p, way], to)

    def ring_2(p, way, src, dst, out, came):
        flag = reduce_flag(p)
        first, second = me.axes(flag)
        to = me.dp_of(flag, first, around(second, 1 - 2 * way))
        return send(src.at[p, way], dst.at[p, way], out, came.at[p, way], to)

    def s1(p, way):
        return ring_1(p, way, s1s, s1r, s1_out, s1_in)

    def s2(p, way):
        return ring_1(p, way, s2s, s2r, s2_out, s2_in)

    def z1(p, way):
        return ring_2(p, way, z1s, z1r, z1_out, z1_in)

    def z2(p, way):
        return ring_2(p, way, z2s, z2r, z2_out, z2_in)

    def stage_a(p):
        flag = reduce_flag(p)
        far = partial(p, flag, around(me.axes(flag)[0], 2)).astype(BF)
        for way in (0, 1):
            s1s[p, way] = far[:, 128 * way : 128 * way + 128]
            s1(p, way).start()

    def stage_b(p):
        flag = reduce_flag(p)
        for way in (0, 1):
            near = partial(p, flag, around(me.axes(flag)[0], 1 - 2 * way))
            s1(p, way).wait_recv()
            for half in (0, 1):
                value = near[:, 128 * half : 128 * half + 128]
                if half == way:
                    value = value + s1r[p, way].astype(F32)
                s2s[p, way, half] = value.astype(BF)
            s2(p, way).start()

    def stage_c(p):
        flag = reduce_flag(p)
        first, second = me.axes(flag)
        own = partial(p, flag, first)
        s2(p, 0).wait_recv()
        s2(p, 1).wait_recv()
        for half in (0, 1):
            value = own[:, 128 * half : 128 * half + 128]
            value = value + s2r[p, 0, half].astype(F32) + s2r[p, 1, half].astype(F32)
            T[p, half] = value.reshape(4, 48, 128)
        for way in (0, 1):
            z1s[p, way] = T[p, way, around(second, 2)].astype(BF)
            z1(p, way).start()

    def stage_d(p):
        second = me.axes(reduce_flag(p))[1]
        for way in (0, 1):
            z1(p, way).wait_recv()
            for half in (0, 1):
                value = T[p, half, around(second, 1 - 2 * way)]
                if half == way:
                    value = value + z1r[p, way].astype(F32)
                z2s[p, way, half] = value.astype(BF)
            z2(p, way).start()

    def stage_e(p):
        second = me.axes(reduce_flag(p))[1]
        z2(p, 0).wait_recv()
        z2(p, 1).wait_recv()
        halves = [
            T[p, half, second] + z2r[p, 0, half].astype(F32) + z2r[p, 1, half].astype(F32) for half in (0, 1)
        ]
        total = jnp.concatenate(halves, axis=1)

        @pl.when(p < NQ)
        def _():
            RA[p] = inner_hadamard(total, had[...])

        @pl.when(p >= NQ)
        def _():
            GU[p - NQ] = total

    def outer(own, came, half_1, came_1, half_2, came_2, x_sem, in_sem, out_sem):
        def x_copy(k):
            return send(own, came.at[k - 1], out_sem.at[k - 1], x_sem.at[k - 1], me.to_x(k))

        core_copy = send(half_1, came_1, out_sem.at[3], in_sem.at[0], me.to_core())
        zl_copy = send(half_2, came_2, out_sem.at[4], in_sem.at[1], me.to_zl())

        def start():
            for k in (1, 2, 3):
                x_copy(k).start()

        def along_x(inner):
            for k in (1, 2, 3):
                x_copy(k).wait_recv()

            @pl.loop(0, NQ)
            def _(q):
                total = x_sign(me, me.x) * own[q]
                for k in (1, 2, 3):
                    total = total + x_sign(me, me.at_x(-k)) * came[k - 1, q]
                half_1[q] = inner(total)

            core_copy.start()

        def cores():
            core_copy.wait_recv()

            @pl.loop(0, NQ)
            def _(q):
                half_2[q] = came_1[q] + sign_of(me.core) * half_1[q]

            zl_copy.start()

        def along_zl(store):
            zl_copy.wait_recv()

            @pl.loop(0, NQ)
            def _(q):
                store(q, (came_2[q] + sign_of(me.zl) * half_2[q]) * (1.0 / math.sqrt(BLK * 16)))

        def finish():
            for k in (1, 2, 3):
                x_copy(k).wait_send()
            core_copy.wait_send()
            zl_copy.wait_send()

        return start, along_x, cores, along_zl, finish

    rot = outer(RA, RX, RB, RC, RD, RE, rx_in, r_in, r_out)
    hid = outer(HID, HX, HB, HC, HD, HE, hx_in, h_in, h_out)

    def gathering(buf, row, flag_of):
        def place(u):
            flag = flag_of(u)
            return flag, *me.axes(flag)

        def second_copy(u, way, at, half=None):
            flag, first, second = place(u)
            part = slice(None) if half is None else half
            ref = buf.at[u, part, 4 * first + at]
            sem = (a2f if half is None else a2h).at[row + u, way]
            return send(ref, ref, ag_out.at[row // NQ], sem, me.dp_of(flag, first, around(second, 1 - 2 * way)))

        def first_copy(u, way, at, half=None):
            flag, first, second = place(u)
            part = slice(None) if half is None else half
            ref = buf.at[u, part, pl.ds(4 * at, 4)]
            sem = (a1f if half is None else a1h).at[row + u, way]
            return send(ref, ref, ag_out.at[row // NQ], sem, me.dp_of(flag, around(first, 1 - 2 * way), second))

        def along_first(u, at):
            flag, first, second = place(u)
            ref = buf.at[u, :, 4 * first + at]
            for way in (0, 1):
                to = me.dp_of(flag, around(first, 1 - 2 * way), second)
                send(ref, ref, ag_out.at[row // NQ], a1f.at[row + u, way], to).start()

        def begin(u):
            for way in (0, 1):
                second_copy(u, way, place(u)[2]).start()
            along_first(u, place(u)[2])

        def pass_second(u):
            for way in (0, 1):
                at = around(place(u)[2], 2 * way - 1)
                second_copy(u, way, at).wait_recv()
                second_copy(u, way, at, way).start()
                along_first(u, at)

        def begin_first(u):
            for way in (0, 1):
                second_copy(u, way, around(place(u)[2], 2), way).wait_recv()
            along_first(u, around(place(u)[2], 2))

        def pass_first(u):
            for way in (0, 1):
                at = around(place(u)[1], 2 * way - 1)
                first_copy(u, way, at).wait_recv()
                first_copy(u, way, at, way).start()

        def complete(u):
            for way in (0, 1):
                first_copy(u, way, around(place(u)[1], 2), way).wait_recv()

        def finish():
            sent = buf.at[:, :, pl.ds(0, 15)]
            send(sent, sent, ag_out.at[row // NQ], a2f.at[0, 0], me.to_zl()).wait_send()

        return begin, pass_second, begin_first, pass_first, complete, finish

    def own_position(flag):
        first, second = me.axes(flag)
        return 4 * first + second

    def in_order(flag, block):
        halves = []
        for half in (0, 1):
            rows = [block(half, (4 - 3 * flag) * (d // 4) + (1 + 3 * flag) * (d % 4)) for d in range(16)]
            halves.append(jnp.concatenate(rows, axis=0))
        return jnp.concatenate(halves, axis=1)

    grads = gathering(AG, 0, grads_flag)
    turned = gathering(AR, NQ, rotated_flag)

    def grads_begin(q):
        gate, up, d_hidden = GU[2 * q], GU[2 * q + 1], DH[q]
        sigma = jax.nn.sigmoid(gate)
        silu_gate = gate * sigma
        HID[q] = silu_gate * up
        pair = (
            (d_hidden * up * sigma * (1.0 + gate * (1.0 - sigma))).astype(BF),
            (d_hidden * silu_gate).astype(BF),
        )
        at = own_position(grads_flag(q))
        for s in (0, 1):
            for half in (0, 1):
                AG[q, half, at, s] = pair[s][:, 128 * half : 128 * half + 128]
        grads[0](q)

    def out_grad(q, s):
        to = (DG, DU)[s].at[:, pl.ds(pl.multiple_of(256 * q, 256), 256)]
        return pltpu.make_async_copy(OW.at[q, s], to, o_sem.at[q, s])

    def out_down(q):
        to = DD.at[pl.ds(pl.multiple_of(256 * q, 256), 256)]
        return pltpu.make_async_copy(OD.at[q], to, o_sem.at[q, 2])

    def grads_end(q):
        grads[4](q)
        flag = grads_flag(q)
        total = None
        for s in (0, 1):
            value = in_order(flag, lambda half, at: AG[q, half, at, s])
            OW[q, s] = jnp.dot(XT[...], value, preferred_element_type=F32).astype(BF)
            out_grad(q, s).start()
            term = lax.dot_general(
                value, W[NQ + 2 * q + s], (((1,), (1,)), ((), ())), preferred_element_type=F32
            )
            total = term if total is None else total + term
        for n in range(16):
            PT[n % 2, n // 2] += total[48 * n : 48 * n + 48]

    def rotated_store(q, value):
        at = own_position(rotated_flag(q))
        for half in (0, 1):
            AR[q, half, at] = value[:, 128 * half : 128 * half + 128].astype(BF)
        turned[0](q)

    def rotated_end(q):
        turned[4](q)
        value = in_order(rotated_flag(q), lambda half, at: AR[q, half, at])
        OD[q] = jnp.dot(value.T, X[0].reshape(768, 512), preferred_element_type=F32).astype(BF)
        out_down(q).start()

    sum_core = send(PT.at[1 - me.core], PR, t_out.at[0], core_in, me.to_core())
    sum_zl = send(SZ.at[1 - me.zl], ZR, t_out.at[1], zl_in, me.to_zl())

    def sum_x(k, zl):
        return send(
            PR.at[4 * zl + me.at_x(k)], XR.at[k - 1, zl], x_out.at[k - 1, zl], x_in.at[k - 1, zl], me.to_x(k)
        )

    def sum_1():
        sum_core.wait_recv()
        for j in range(8):
            PR[j] = PR[j] + PT[me.core, j]
        for k in (1, 2, 3):
            for zl in (0, 1):
                sum_x(k, zl).start()

    def sum_2():
        for k in (1, 2, 3):
            for zl in (0, 1):
                sum_x(k, zl).wait_recv()
        for zl in (0, 1):
            SZ[zl] = PR[4 * zl + me.x] + XR[0, zl] + XR[1, zl] + XR[2, zl]
        sum_zl.start()

    def store_d_hidden(q, value):
        DH[q] = value

    at_step = {
        1: lambda: gather_x(1),
        3: lambda: gather_core(1),
        ROT_X: rot[0],
        ROT_CORE: lambda: rot[1](lambda value: value),
        ROT_ZL: rot[2],
        ROT_END: lambda: rot[3](store_d_hidden),
        HID_CORE: lambda: hid[1](lambda value: inner_hadamard(value, had[...])),
        HID_ZL: hid[2],
        HID_END: lambda: hid[3](rotated_store),
        SUM_X: sum_1,
        SUM_ZL: sum_2,
    }
    stages = [(stage_a, 0, NP), (stage_b, LAG_B, NP), (stage_c, LAG_C, NP), (stage_d, LAG_D, NP), (stage_e, LAG_E, NP)]
    stages += [(grads_begin, GRADS, NQ)]
    stages += [(grads[n], GRADS + SPREAD[n], NQ) for n in (1, 2, 3)]
    stages += [(turned[n], HID_END + SPREAD[n], NQ) for n in (1, 2, 3)]
    stages += [(grads_end, GRADS + SPREAD[4], NQ), (rotated_end, HID_END + SPREAD[4], NQ)]

    @pl.loop(0, STEPS)
    def _(i):
        for step, work in at_step.items():
            pl.when(i == step)(work)
        for stage, first, count in stages:

            @pl.when((i >= first) & (i < first + count))
            def _(stage=stage, first=first):
                stage(i - first)

        @pl.when(i == 5)
        def _():
            XT[...] = X[1].reshape(768, 512).T

        pl.when(i == HID_X)(hid[0])
        pl.when(i == GRADS + SPREAD[4] + NQ - 1)(sum_core.start)

    sum_zl.wait_recv()
    DT[...] = (SZ[me.zl] + ZR[...]).astype(BF)
    for q in range(NQ):
        for s in (0, 1):
            out_grad(q, s).wait()
        out_down(q).wait()
    for s in (0, 1):
        sent = X.at[s, pl.ds(0, 15)]
        send(sent, sent, gs.at[s], gz.at[s], me.to_zl()).wait_send()
    for src, dst, out in ((s1s, s1r, s1_out), (s2s, s2r, s2_out), (z1s, z1r, z1_out), (z2s, z2r, z2_out)):
        send(src, dst, out, gz.at[0], me.to_zl()).wait_send()
    rot[4]()
    hid[4]()
    grads[5]()
    turned[5]()
    sum_core.wait_send()
    sum_zl.wait_send()
    for k in (1, 2, 3):
        for zl in (0, 1):
            sum_x(k, zl).wait_send()


def per_device(tokens, w_gate, w_up, w_down, cotangent):
    whole = pl.BlockSpec(memory_space=pltpu.VMEM)
    any_space = pl.BlockSpec(memory_space=pl.ANY)
    dma = pltpu.SemaphoreType.DMA
    part = pltpu.VMEM((NQ, 48, 256), F32)
    d_gate, d_up, d_down, d_tokens = pl.pallas_call(
        layer_kernel,
        out_shape=(
            jax.ShapeDtypeStruct((512, 1792), BF),
            jax.ShapeDtypeStruct((512, 1792), BF),
            jax.ShapeDtypeStruct((1792, 512), BF),
            jax.ShapeDtypeStruct((48, 512), BF),
        ),
        in_specs=[whole, whole, any_space, any_space, any_space, whole],
        out_specs=(any_space, any_space, any_space, whole),
        scratch_shapes=[
            pltpu.VMEM((2, 16, 48, 512), BF),
            pltpu.VMEM((512, 768), BF),
            pltpu.VMEM((NP, 512, 256), BF),
            pltpu.VMEM((1792, 512), BF),
            pltpu.VMEM((NP, 2, 192, 128), BF),
            pltpu.VMEM((NP, 2, 192, 128), BF),
            pltpu.VMEM((NP, 2, 2, 192, 128), BF),
            pltpu.VMEM((NP, 2, 2, 192, 128), BF),
            pltpu.VMEM((NP, 2, 4, 48, 128), F32),
            pltpu.VMEM((NP, 2, 48, 128), BF),
            pltpu.VMEM((NP, 2, 48, 128), BF),
            pltpu.VMEM((NP, 2, 2, 48, 128), BF),
            pltpu.VMEM((NP, 2, 2, 48, 128), BF),
            pltpu.VMEM((2 * NQ, 48, 256), F32),
            part,
            part, pltpu.VMEM((3, NQ, 48, 256), F32), part, part, part, part,
            part, pltpu.VMEM((3, NQ, 48, 256), F32), part, part, part, part,
            pltpu.VMEM((NQ, 2, 16, 2, 48, 128), BF),
            pltpu.VMEM((NQ, 2, 16, 48, 128), BF),
            pltpu.VMEM((NQ, 2, 512, 256), BF),
            pltpu.VMEM((NQ, 256, 512), BF),
            pltpu.VMEM((2, 8, 48, 512), F32),
            pltpu.VMEM((8, 48, 512), F32),
            pltpu.VMEM((3, 2, 48, 512), F32),
            pltpu.VMEM((2, 48, 512), F32),
            pltpu.VMEM((48, 512), F32),
            dma((15,)), dma((2,)), dma((2, 2, 3)), dma((2, 8)), dma((2,)),
            dma, dma((NP, 2)), dma, dma((NP, 2)), dma, dma((NP, 2)), dma, dma((NP, 2)),
            dma((3,)), dma((2,)), dma((5,)), dma((3,)), dma((2,)), dma((5,)),
            dma((2,)), dma((2 * NQ, 2)), dma((2 * NQ, 2)), dma((2 * NQ, 2)), dma((2 * NQ, 2)),
            dma, dma((3, 2)), dma, dma((2,)), dma((3, 2)), dma((NQ, 3)),
        ],
        compiler_params=pltpu.CompilerParams(
            collective_id=0, has_side_effects=True, vmem_limit_bytes=60 * 1024 * 1024
        ),
        name="layer_backward",
    )(tokens, cotangent, w_gate, w_up, w_down, sylvester(BLK, BF))
    return (d_tokens, d_gate, d_up, d_down)


def solution(mesh):
    return jax.shard_map(
        per_device,
        mesh=mesh,
        in_specs=(
            P("tensor", "dp"),
            P("dp", "tensor"),
            P("dp", "tensor"),
            P("tensor", "dp"),
            P("tensor", "dp"),
        ),
        out_specs=(P("tensor", "dp"), P("dp", "tensor"), P("dp", "tensor"), P("tensor", "dp")),
        check_vma=False,
    )
```

```python
import functools
import math

import jax
import jax.numpy as jnp
from jax import lax
from jax.experimental import pallas as pl
from jax.experimental.pallas import tpu as pltpu
from jax.sharding import PartitionSpec as P

BLK = 128
BF = jnp.bfloat16
F32 = jnp.float32
MESH = pl.DeviceIdType.MESH
NQ = 7
NP = 3 * NQ
LAG_B, LAG_C, LAG_D, LAG_E = 3, 6, 9, 12
ROT_X, ROT_CORE, ROT_ZL, ROT_END = 19, 24, 26, 29
GRADS = 29
HID_X, HID_CORE, HID_ZL, HID_END = 35, 38, 41, 44
SPREAD = (0, 4, 8, 14, 18)
SUM_X, SUM_ZL = 54, 58
STEPS = HID_END + SPREAD[4] + NQ


def reduce_flag(p):
    return jnp.where(lax.rem(p, 4) == 3, 1, 0)


def grads_flag(q):
    return jnp.where(q == 3, 1, 0)


def rotated_flag(q):
    return jnp.where(q == 3, 1, 0)


def sylvester(order, dtype=jnp.float32):
    positions = jnp.arange(order, dtype=jnp.int32)
    row_ids = positions[:, None]
    col_ids = positions[None, :]
    signs = jnp.ones((order, order), jnp.float32)
    for power in range(order.bit_length() - 1):
        both = (row_ids >> power & 1) * (col_ids >> power & 1)
        signs = signs * (1 - 2 * both).astype(jnp.float32)
    return signs.astype(dtype)


def around(position, step):
    return lax.rem(position + step + 4, 4)


class Place:
    def __init__(self):
        self.dp = lax.axis_index("dp")
        self.t = lax.axis_index("tensor")
        self.y, self.zh = lax.div(self.dp, 4), lax.rem(self.dp, 4)
        self.zl = lax.div(self.t, 8)
        self.x = lax.rem(lax.div(self.t, 2), 4)
        self.core = lax.rem(self.t, 2)

    def axes(self, flag):
        return self.y + flag * (self.zh - self.y), self.zh + flag * (self.y - self.zh)

    def dp_of(self, flag, first, second):
        return {"dp": (4 - 3 * flag) * first + (1 + 3 * flag) * second, "tensor": self.t}

    def at_x(self, step):
        return lax.rem(self.x + step + 4, 4)

    def slot(self, zl, x, core):
        return zl * 8 + x * 2 + core

    def to_x(self, step):
        return {"dp": self.dp, "tensor": self.slot(self.zl, self.at_x(step), self.core)}

    def to_core(self):
        return {"dp": self.dp, "tensor": self.slot(self.zl, self.x, 1 - self.core)}

    def to_zl(self):
        return {"dp": self.dp, "tensor": self.slot(1 - self.zl, self.x, self.core)}

    def meet(self):
        peers = []
        for step in (1, -1):
            peers.append(self.dp_of(0, around(self.y, step), self.zh))
            peers.append(self.dp_of(0, self.y, around(self.zh, step)))
        peers += [self.to_x(k) for k in (1, 2, 3)] + [self.to_core(), self.to_zl()]
        barrier = pltpu.get_barrier_semaphore()
        for peer in peers:
            pl.semaphore_signal(barrier, inc=1, device_id=peer, device_id_type=MESH)
        pl.semaphore_wait(barrier, len(peers))


def send(src, dst, send_sem, recv_sem, to):
    return pltpu.make_async_remote_copy(
        src_ref=src, dst_ref=dst, send_sem=send_sem, recv_sem=recv_sem, device_id=to, device_id_type=MESH
    )


def sign_of(bit):
    return (1 - 2 * bit).astype(F32)


def x_sign(place, other):
    both = lax.rem(place.x, 2) * lax.rem(other, 2) + lax.div(place.x, 2) * lax.div(other, 2)
    return sign_of(lax.rem(both, 2))


def inner_hadamard(value, had):
    parts = []
    for start in range(0, value.shape[1], BLK):
        block = value[:, start : start + BLK]
        high = block.astype(BF)
        low = (block - high.astype(F32)).astype(BF)
        parts.append(
            jnp.dot(high, had, preferred_element_type=F32) + jnp.dot(low, had, preferred_element_type=F32)
        )
    return jnp.concatenate(parts, axis=1)


def layer_kernel(
    tok, cot, wg, wu, wd, had,
    DG, DU, DD, DT,
    X, XT, W, WD, s1s, s1r, s2s, s2r, T, z1s, z1r, z2s, z2r, GU, DH,
    RA, RX, RB, RC, RD, RE, HID, HX, HB, HC, HD, HE, AG, AR, OW, OD, PT, PR, XR, SZ, ZR,
    load_sem, gz, gx, gc, gs, s1_out, s1_in, s2_out, s2_in, z1_out, z1_in, z2_out, z2_in,
    rx_in, r_in, r_out, hx_in, h_in, h_out, ag_out, a2f, a2h, a1f, a1h, core_in, x_in, zl_in, t_out, x_out, o_sem,
):
    me = Place()
    loads = [pltpu.make_async_copy(wd, WD, load_sem.at[0])]
    for q in range(NQ):
        loads.append(pltpu.make_async_copy(wg.at[:, pl.ds(256 * q, 256)], W.at[NQ + 2 * q], load_sem.at[1 + q]))
        loads.append(pltpu.make_async_copy(wu.at[:, pl.ds(256 * q, 256)], W.at[NQ + 2 * q + 1], load_sem.at[1 + NQ + q]))
    for load in loads:
        load.start()
    me.meet()

    other = me.slot(1 - me.zl, me.x, me.core)

    def gather_own(s, own):
        X[s, me.t] = own[...]
        send(X.at[s, me.t], X.at[s, me.t], gs.at[s], gz.at[s], me.to_zl()).start()
        for k in (1, 2, 3):
            send(X.at[s, me.t], X.at[s, me.t], gs.at[s], gx.at[s, 0, k - 1], me.to_x(k)).start()

    def gather_zl(s):
        send(X.at[s, other], X.at[s, other], gs.at[s], gz.at[s], me.to_zl()).wait_recv()
        for k in (1, 2, 3):
            send(X.at[s, other], X.at[s, other], gs.at[s], gx.at[s, 1, k - 1], me.to_x(k)).start()

    def to_core(s, zl, x, n):
        block = X.at[s, me.slot(zl, x, me.core)]
        send(block, block, gs.at[s], gc.at[s, n], me.to_core()).start()

    def gather_x(s):
        to_core(s, me.zl, me.x, 0)
        to_core(s, 1 - me.zl, me.x, 4)
        for j, zl in ((0, me.zl), (1, 1 - me.zl)):
            for k in (1, 2, 3):
                came = me.at_x(-k)
                block = X.at[s, me.slot(zl, came, me.core)]
                send(block, block, gs.at[s], gx.at[s, j, k - 1], me.to_x(k)).wait_recv()
                to_core(s, zl, came, 4 * j + k)

    def gather_core(s):
        for j, zl in ((0, me.zl), (1, 1 - me.zl)):
            for k in range(4):
                block = X.at[s, me.slot(zl, me.at_x(-k), 1 - me.core)]
                send(block, block, gs.at[s], gc.at[s, 4 * j + k], me.to_core()).wait_recv()

    gather_own(0, cot)
    loads[0].wait()
    for q in range(3):
        W[q] = WD[pl.ds(256 * q, 256), :].T
    gather_zl(0)
    gather_own(1, tok)
    for q in range(3, NQ):
        W[q] = WD[pl.ds(256 * q, 256), :].T
    gather_zl(1)
    PT[...] = jnp.zeros_like(PT)
    gather_x(0)
    gather_core(0)
    for load in loads[1:]:
        load.wait()

    def partial(p, flag, first):
        s = jnp.where(p < NQ, 0, 1)
        rows = [X[s, (4 - 3 * flag) * first + (1 + 3 * flag) * j] for j in range(4)]
        return jnp.dot(jnp.concatenate(rows, axis=0), W[p], preferred_element_type=F32)

    def ring_1(p, way, src, dst, out, came):
        flag = reduce_flag(p)
        first, second = me.axes(flag)
        to = me.dp_of(flag, around(first, 1 - 2 * way), second)
        return send(src.at[p, way], dst.at[p, way], out, came.at[p, way], to)

    def ring_2(p, way, src, dst, out, came):
        flag = reduce_flag(p)
        first, second = me.axes(flag)
        to = me.dp_of(flag, first, around(second, 1 - 2 * way))
        return send(src.at[p, way], dst.at[p, way], out, came.at[p, way], to)

    def s1(p, way):
        return ring_1(p, way, s1s, s1r, s1_out, s1_in)

    def s2(p, way):
        return ring_1(p, way, s2s, s2r, s2_out, s2_in)

    def z1(p, way):
        return ring_2(p, way, z1s, z1r, z1_out, z1_in)

    def z2(p, way):
        return ring_2(p, way, z2s, z2r, z2_out, z2_in)

    def stage_a(p):
        flag = reduce_flag(p)
        far = partial(p, flag, around(me.axes(flag)[0], 2)).astype(BF)
        for way in (0, 1):
            s1s[p, way] = far[:, 128 * way : 128 * way + 128]
            s1(p, way).start()

    def stage_b(p):
        flag = reduce_flag(p)
        for way in (0, 1):
            near = partial(p, flag, around(me.axes(flag)[0], 1 - 2 * way))
            s1(p, way).wait_recv()
            for half in (0, 1):
                value = near[:, 128 * half : 128 * half + 128]
                if half == way:
                    value = value + s1r[p, way].astype(F32)
                s2s[p, way, half] = value.astype(BF)
            s2(p, way).start()

    def stage_c(p):
        flag = reduce_flag(p)
        first, second = me.axes(flag)
        own = partial(p, flag, first)
        s2(p, 0).wait_recv()
        s2(p, 1).wait_recv()
        for half in (0, 1):
            value = own[:, 128 * half : 128 * half + 128]
            value = value + s2r[p, 0, half].astype(F32) + s2r[p, 1, half].astype(F32)
            T[p, half] = value.reshape(4, 48, 128)
        for way in (0, 1):
            z1s[p, way] = T[p, way, around(second, 2)].astype(BF)
            z1(p, way).start()

    def stage_d(p):
        second = me.axes(reduce_flag(p))[1]
        for way in (0, 1):
            z1(p, way).wait_recv()
            for half in (0, 1):
                value = T[p, half, around(second, 1 - 2 * way)]
                if half == way:
                    value = value + z1r[p, way].astype(F32)
                z2s[p, way, half] = value.astype(BF)
            z2(p, way).start()

    def stage_e(p):
        second = me.axes(reduce_flag(p))[1]
        z2(p, 0).wait_recv()
        z2(p, 1).wait_recv()
        halves = [
            T[p, half, second] + z2r[p, 0, half].astype(F32) + z2r[p, 1, half].astype(F32) for half in (0, 1)
        ]
        total = jnp.concatenate(halves, axis=1)

        @pl.when(p < NQ)
        def _():
            RA[p] = inner_hadamard(total, had[...])

        @pl.when(p >= NQ)
        def _():
            GU[p - NQ] = total

    def outer(own, came, half_1, came_1, half_2, came_2, x_sem, in_sem, out_sem):
        def x_copy(k):
            return send(own, came.at[k - 1], out_sem.at[k - 1], x_sem.at[k - 1], me.to_x(k))

        core_copy = send(half_1, came_1, out_sem.at[3], in_sem.at[0], me.to_core())
        zl_copy = send(half_2, came_2, out_sem.at[4], in_sem.at[1], me.to_zl())

        def start():
            for k in (1, 2, 3):
                x_copy(k).start()

        def along_x(inner):
            for k in (1, 2, 3):
                x_copy(k).wait_recv()

            @pl.loop(0, NQ)
            def _(q):
                total = x_sign(me, me.x) * own[q]
                for k in (1, 2, 3):
                    total = total + x_sign(me, me.at_x(-k)) * came[k - 1, q]
                half_1[q] = inner(total)

            core_copy.start()

        def cores():
            core_copy.wait_recv()

            @pl.loop(0, NQ)
            def _(q):
                half_2[q] = came_1[q] + sign_of(me.core) * half_1[q]

            zl_copy.start()

        def along_zl(store):
            zl_copy.wait_recv()

            @pl.loop(0, NQ)
            def _(q):
                store(q, (came_2[q] + sign_of(me.zl) * half_2[q]) * (1.0 / math.sqrt(BLK * 16)))

        def finish():
            for k in (1, 2, 3):
                x_copy(k).wait_send()
            core_copy.wait_send()
            zl_copy.wait_send()

        return start, along_x, cores, along_zl, finish

    rot = outer(RA, RX, RB, RC, RD, RE, rx_in, r_in, r_out)
    hid = outer(HID, HX, HB, HC, HD, HE, hx_in, h_in, h_out)

    def gathering(buf, row, flag_of):
        def place(u):
            flag = flag_of(u)
            return flag, *me.axes(flag)

        def second_copy(u, way, at, half=None):
            flag, first, second = place(u)
            part = slice(None) if half is None else half
            ref = buf.at[u, part, 4 * first + at]
            sem = (a2f if half is None else a2h).at[row + u, way]
            return send(ref, ref, ag_out.at[row // NQ], sem, me.dp_of(flag, first, around(second, 1 - 2 * way)))

        def first_copy(u, way, at, half=None):
            flag, first, second = place(u)
            part = slice(None) if half is None else half
            ref = buf.at[u, part, pl.ds(4 * at, 4)]
            sem = (a1f if half is None else a1h).at[row + u, way]
            return send(ref, ref, ag_out.at[row // NQ], sem, me.dp_of(flag, around(first, 1 - 2 * way), second))

        def along_first(u, at):
            flag, first, second = place(u)
            ref = buf.at[u, :, 4 * first + at]
            for way in (0, 1):
                to = me.dp_of(flag, around(first, 1 - 2 * way), second)
                send(ref, ref, ag_out.at[row // NQ], a1f.at[row + u, way], to).start()

        def begin(u):
            for way in (0, 1):
                second_copy(u, way, place(u)[2]).start()
            along_first(u, place(u)[2])

        def pass_second(u):
            for way in (0, 1):
                at = around(place(u)[2], 2 * way - 1)
                second_copy(u, way, at).wait_recv()
                second_copy(u, way, at, way).start()
                along_first(u, at)

        def begin_first(u):
            for way in (0, 1):
                second_copy(u, way, around(place(u)[2], 2), way).wait_recv()
            along_first(u, around(place(u)[2], 2))

        def pass_first(u):
            for way in (0, 1):
                at = around(place(u)[1], 2 * way - 1)
                first_copy(u, way, at).wait_recv()
                first_copy(u, way, at, way).start()

        def complete(u):
            for way in (0, 1):
                first_copy(u, way, around(place(u)[1], 2), way).wait_recv()

        def finish():
            sent = buf.at[:, :, pl.ds(0, 15)]
            send(sent, sent, ag_out.at[row // NQ], a2f.at[0, 0], me.to_zl()).wait_send()

        return begin, pass_second, begin_first, pass_first, complete, finish

    def own_position(flag):
        first, second = me.axes(flag)
        return 4 * first + second

    def in_order(flag, block):
        halves = []
        for half in (0, 1):
            rows = [block(half, (4 - 3 * flag) * (d // 4) + (1 + 3 * flag) * (d % 4)) for d in range(16)]
            halves.append(jnp.concatenate(rows, axis=0))
        return jnp.concatenate(halves, axis=1)

    grads = gathering(AG, 0, grads_flag)
    turned = gathering(AR, NQ, rotated_flag)

    def grads_begin(q):
        gate, up, d_hidden = GU[2 * q], GU[2 * q + 1], DH[q]
        sigma = jax.nn.sigmoid(gate)
        silu_gate = gate * sigma
        HID[q] = silu_gate * up
        pair = (
            (d_hidden * up * sigma * (1.0 + gate * (1.0 - sigma))).astype(BF),
            (d_hidden * silu_gate).astype(BF),
        )
        at = own_position(grads_flag(q))
        for s in (0, 1):
            for half in (0, 1):
                AG[q, half, at, s] = pair[s][:, 128 * half : 128 * half + 128]
        grads[0](q)

    def out_grad(q, s):
        to = (DG, DU)[s].at[:, pl.ds(pl.multiple_of(256 * q, 256), 256)]
        return pltpu.make_async_copy(OW.at[q, s], to, o_sem.at[q, s])

    def out_down(q):
        to = DD.at[pl.ds(pl.multiple_of(256 * q, 256), 256)]
        return pltpu.make_async_copy(OD.at[q], to, o_sem.at[q, 2])

    def grads_end(q):
        grads[4](q)
        flag = grads_flag(q)
        total = None
        for s in (0, 1):
            value = in_order(flag, lambda half, at: AG[q, half, at, s])
            OW[q, s] = jnp.dot(XT[...], value, preferred_element_type=F32).astype(BF)
            out_grad(q, s).start()
            term = lax.dot_general(
                value, W[NQ + 2 * q + s], (((1,), (1,)), ((), ())), preferred_element_type=F32
            )
            total = term if total is None else total + term
        for n in range(16):
            PT[n % 2, n // 2] += total[48 * n : 48 * n + 48]

    def rotated_store(q, value):
        at = own_position(rotated_flag(q))
        for half in (0, 1):
            AR[q, half, at] = value[:, 128 * half : 128 * half + 128].astype(BF)
        turned[0](q)

    def rotated_end(q):
        turned[4](q)
        value = in_order(rotated_flag(q), lambda half, at: AR[q, half, at])
        OD[q] = jnp.dot(value.T, X[0].reshape(768, 512), preferred_element_type=F32).astype(BF)
        out_down(q).start()

    sum_core = send(PT.at[1 - me.core], PR, t_out.at[0], core_in, me.to_core())
    sum_zl = send(SZ.at[1 - me.zl], ZR, t_out.at[1], zl_in, me.to_zl())

    def sum_x(k, zl):
        return send(
            PR.at[4 * zl + me.at_x(k)], XR.at[k - 1, zl], x_out.at[k - 1, zl], x_in.at[k - 1, zl], me.to_x(k)
        )

    def sum_1():
        sum_core.wait_recv()
        for j in range(8):
            PR[j] = PR[j] + PT[me.core, j]
        for k in (1, 2, 3):
            for zl in (0, 1):
                sum_x(k, zl).start()

    def sum_2():
        for k in (1, 2, 3):
            for zl in (0, 1):
                sum_x(k, zl).wait_recv()
        for zl in (0, 1):
            SZ[zl] = PR[4 * zl + me.x] + XR[0, zl] + XR[1, zl] + XR[2, zl]
        sum_zl.start()

    def store_d_hidden(q, value):
        DH[q] = value

    at_step = {
        1: lambda: gather_x(1),
        3: lambda: gather_core(1),
        ROT_X: rot[0],
        ROT_CORE: lambda: rot[1](lambda value: value),
        ROT_ZL: rot[2],
        ROT_END: lambda: rot[3](store_d_hidden),
        HID_CORE: lambda: hid[1](lambda value: inner_hadamard(value, had[...])),
        HID_ZL: hid[2],
        HID_END: lambda: hid[3](rotated_store),
        SUM_X: sum_1,
        SUM_ZL: sum_2,
    }
    stages = [(stage_a, 0, NP), (stage_b, LAG_B, NP), (stage_c, LAG_C, NP), (stage_d, LAG_D, NP), (stage_e, LAG_E, NP)]
    stages += [(grads_begin, GRADS, NQ)]
    stages += [(grads[n], GRADS + SPREAD[n], NQ) for n in (1, 2, 3)]
    stages += [(turned[n], HID_END + SPREAD[n], NQ) for n in (1, 2, 3)]
    stages += [(grads_end, GRADS + SPREAD[4], NQ), (rotated_end, HID_END + SPREAD[4], NQ)]

    @pl.loop(0, STEPS)
    def _(i):
        for step, work in at_step.items():
            pl.when(i == step)(work)
        for stage, first, count in stages:

            @pl.when((i >= first) & (i < first + count))
            def _(stage=stage, first=first):
                stage(i - first)

        @pl.when(i == 5)
        def _():
            XT[...] = X[1].reshape(768, 512).T

        pl.when(i == HID_X)(hid[0])
        pl.when(i == GRADS + SPREAD[4] + NQ - 1)(sum_core.start)

    sum_zl.wait_recv()
    DT[...] = (SZ[me.zl] + ZR[...]).astype(BF)
    for q in range(NQ):
        for s in (0, 1):
            out_grad(q, s).wait()
        out_down(q).wait()
    for s in (0, 1):
        sent = X.at[s, pl.ds(0, 15)]
        send(sent, sent, gs.at[s], gz.at[s], me.to_zl()).wait_send()
    for src, dst, out in ((s1s, s1r, s1_out), (s2s, s2r, s2_out), (z1s, z1r, z1_out), (z2s, z2r, z2_out)):
        send(src, dst, out, gz.at[0], me.to_zl()).wait_send()
    rot[4]()
    hid[4]()
    grads[5]()
    turned[5]()
    sum_core.wait_send()
    sum_zl.wait_send()
    for k in (1, 2, 3):
        for zl in (0, 1):
            sum_x(k, zl).wait_send()


def per_device(tokens, w_gate, w_up, w_down, cotangent):
    whole = pl.BlockSpec(memory_space=pltpu.VMEM)
    any_space = pl.BlockSpec(memory_space=pl.ANY)
    dma = pltpu.SemaphoreType.DMA
    part = pltpu.VMEM((NQ, 48, 256), F32)
    d_gate, d_up, d_down, d_tokens = pl.pallas_call(
        layer_kernel,
        out_shape=(
            jax.ShapeDtypeStruct((512, 1792), BF),
            jax.ShapeDtypeStruct((512, 1792), BF),
            jax.ShapeDtypeStruct((1792, 512), BF),
            jax.ShapeDtypeStruct((48, 512), BF),
        ),
        in_specs=[whole, whole, any_space, any_space, any_space, whole],
        out_specs=(any_space, any_space, any_space, whole),
        scratch_shapes=[
            pltpu.VMEM((2, 16, 48, 512), BF),
            pltpu.VMEM((512, 768), BF),
            pltpu.VMEM((NP, 512, 256), BF),
            pltpu.VMEM((1792, 512), BF),
            pltpu.VMEM((NP, 2, 192, 128), BF),
            pltpu.VMEM((NP, 2, 192, 128), BF),
            pltpu.VMEM((NP, 2, 2, 192, 128), BF),
            pltpu.VMEM((NP, 2, 2, 192, 128), BF),
            pltpu.VMEM((NP, 2, 4, 48, 128), F32),
            pltpu.VMEM((NP, 2, 48, 128), BF),
            pltpu.VMEM((NP, 2, 48, 128), BF),
            pltpu.VMEM((NP, 2, 2, 48, 128), BF),
            pltpu.VMEM((NP, 2, 2, 48, 128), BF),
            pltpu.VMEM((2 * NQ, 48, 256), F32),
            part,
            part, pltpu.VMEM((3, NQ, 48, 256), F32), part, part, part, part,
            part, pltpu.VMEM((3, NQ, 48, 256), F32), part, part, part, part,
            pltpu.VMEM((NQ, 2, 16, 2, 48, 128), BF),
            pltpu.VMEM((NQ, 2, 16, 48, 128), BF),
            pltpu.VMEM((NQ, 2, 512, 256), BF),
            pltpu.VMEM((NQ, 256, 512), BF),
            pltpu.VMEM((2, 8, 48, 512), F32),
            pltpu.VMEM((8, 48, 512), F32),
            pltpu.VMEM((3, 2, 48, 512), F32),
            pltpu.VMEM((2, 48, 512), F32),
            pltpu.VMEM((48, 512), F32),
            dma((15,)), dma((2,)), dma((2, 2, 3)), dma((2, 8)), dma((2,)),
            dma, dma((NP, 2)), dma, dma((NP, 2)), dma, dma((NP, 2)), dma, dma((NP, 2)),
            dma((3,)), dma((2,)), dma((5,)), dma((3,)), dma((2,)), dma((5,)),
            dma((2,)), dma((2 * NQ, 2)), dma((2 * NQ, 2)), dma((2 * NQ, 2)), dma((2 * NQ, 2)),
            dma, dma((3, 2)), dma, dma((2,)), dma((3, 2)), dma((NQ, 3)),
        ],
        compiler_params=pltpu.CompilerParams(
            collective_id=0, has_side_effects=True, vmem_limit_bytes=60 * 1024 * 1024
        ),
        name="layer_backward",
    )(tokens, cotangent, w_gate, w_up, w_down, sylvester(BLK, BF))
    return (d_tokens, d_gate, d_up, d_down)


def solution(mesh):
    return jax.shard_map(
        per_device,
        mesh=mesh,
        in_specs=(
            P("tensor", "dp"),
            P("dp", "tensor"),
            P("dp", "tensor"),
            P("tensor", "dp"),
            P("tensor", "dp"),
        ),
        out_specs=(P("tensor", "dp"), P("dp", "tensor"), P("dp", "tensor"), P("tensor", "dp")),
        check_vma=False,
    )
```
